32 devices in a mesh: lat: 16 (over z, y, x), field: 2 (over core).
Axes of the slice: x: 2, y: 2, z: 4, core: 2. Of those that a mesh axis runs over, the one named last changes fastest.
Arguments:
- fields_grid: bfloat16 [2, 64, 2, 48, 192], P('field', None, None, 'lat'), may hold values from -6 to 6
- basis: bfloat16 [128, 48, 96], P('lat'), may hold values from -0.875 to 0.875
- order_table: int32 [16, 8], replicated, may hold values from -1 to 95, as said below
- panel_modes: int32 [2, 64], replicated, may hold values from 0 to 95, as said below
Outputs:
- panel: bfloat16 [2, 128, 192, 128], P('field', 'lat')
The draws below stay inside these ranges and needn't reach their ends.
Inputs may be any that keep to these rules, and one draw needn't show every extreme that they name: `order_table`: each order 0 to 95 stands in exactly one slot; every other slot holds -1; some group has all 8 slots filled. `panel_modes`: row 1 is never smaller than row 0 in the same column; degree 95 appears.
All inputs are finite; a program needn't handle non-finite values.
Results may differ from the reference program's by a relative error of at most 0.0082.
Values may be sent and summed in bfloat16 or wider, within the bound.
A program may use at most 64 MiB of HBM per device.

```python
import math
import jax
import jax.numpy as jnp
from jax import lax

SLOTS = 8
SNAP = 64
NMODE = 64
GROUPS = 16
NPAIR = 48
NLON = 192
NORD = 96
LDEG = 96


def draw_order_table(key, part):
    total = GROUPS * SLOTS
    first_key, second_key, third_key = jax.random.split(key, 3)
    full_group = jax.random.randint(first_key, (), 0, GROUPS)
    positions = jax.random.permutation(second_key, total)
    priority = jnp.where(positions // SLOTS == full_group, 0, 1).astype(jnp.int32)
    ordered = positions[jnp.argsort(priority, stable=True)]
    orders = jax.random.permutation(third_key, NORD).astype(jnp.int32)
    flat_table = jnp.full((total,), -1, dtype=jnp.int32).at[ordered[:NORD]].set(orders)
    return flat_table.reshape(GROUPS, SLOTS).astype(jnp.int32)


def draw_panel_modes(key, part):
    first_key, second_key = jax.random.split(key)
    mode_order = jax.random.randint(first_key, (NMODE,), 0, NORD).astype(jnp.int32)
    offset = jax.random.randint(second_key, (NMODE,), 0, LDEG - mode_order).astype(jnp.int32)
    degree = mode_order + offset
    mode_order = mode_order.at[0].set(0).at[1].set(NORD - 1)
    degree = degree.at[0].set(NORD - 1).at[1].set(NORD - 1)
    return jnp.stack([mode_order, degree]).astype(jnp.int32)


def levels(stream_key, extent, cuts, least, top_value):
    def one(axis_at, blocks):
        draws = jax.random.uniform(jax.random.fold_in(jax.random.fold_in(stream_key, 6), axis_at), (blocks,), jnp.float32, least / len(cuts), top_value / len(cuts))
        return jnp.repeat(jnp.exp(draws), extent[axis_at] // blocks).reshape((-1,) + (1,) * (len(extent) - axis_at - 1))

    gain = one(*cuts[0])
    for cut in cuts[1:]:
        gain = gain * one(*cut)
    return gain


def gaussian(stream_key, extent, width, bound, shards=(), kind=jnp.bfloat16):
    loudness = levels(stream_key, extent, shards, -0.22, 0.18) if shards else 1.0
    values = jax.random.normal(stream_key, extent, jnp.float32) * width * loudness
    return jnp.minimum(jnp.maximum(values, -bound), bound).astype(kind)


def setup_inputs(seed: int = 0) -> dict:
    keys = jax.random.split(jax.random.key(seed), 5)
    fields_grid = gaussian(keys[0], (2, SNAP, 2, NPAIR, NLON), 1.0, 6.0, ((0, 2), (3, 16)))
    basis = gaussian(keys[1], (GROUPS * SLOTS, NPAIR, LDEG), NPAIR ** -0.5, 0.875, ((0, 16),))
    order_table = draw_order_table(jax.random.fold_in(keys[4], 71), 0)
    panel_modes = draw_panel_modes(jax.random.fold_in(keys[4], 71), 0)
    return {"fields_grid": fields_grid, "basis": basis, "order_table": order_table, "panel_modes": panel_modes}


def dft_table(orders, lon_count):
    valid_slot = orders >= 0
    safe_orders = jnp.maximum(orders, 0).astype(jnp.int32)
    products = jnp.arange(lon_count, dtype=jnp.int32)[:, None] * safe_orders[None, :] % lon_count
    angles = products.astype(jnp.float32) * (2.0 * math.pi / lon_count)
    cosine = jnp.where(valid_slot[None, :], jnp.cos(angles), 0.0).astype(jnp.bfloat16)
    sine_table = jnp.where(valid_slot[None, :], -jnp.sin(angles), 0.0).astype(jnp.bfloat16)
    return jnp.stack([cosine, sine_table], axis=1)

def field_coefficients(grid_one, basis, orders, dft):
    snap_count = grid_one.shape[0]
    slot_all = orders.shape[0]
    fourier = jnp.einsum('thjn,nrk->hkjrt', grid_one, dft, preferred_element_type=jnp.float32) * (1.0 / math.sqrt(NLON))
    fourier = fourier.reshape(2, slot_all, NPAIR, 2 * snap_count)
    parity_parts = jnp.stack([fourier[0] + fourier[1], fourier[0] - fourier[1]]).astype(jnp.bfloat16)
    degree = jnp.arange(LDEG, dtype=jnp.int32)

    def one_group(index):
        start = (index * SLOTS).astype(jnp.int32)
        basis_block = lax.dynamic_slice_in_dim(basis, start, SLOTS, 0).astype(jnp.float32)
        even_block = lax.dynamic_slice_in_dim(parity_parts[0], start, SLOTS, 0).astype(jnp.float32)
        odd_block = lax.dynamic_slice_in_dim(parity_parts[1], start, SLOTS, 0).astype(jnp.float32)
        group_orders = lax.dynamic_slice_in_dim(orders, start, SLOTS, 0)
        even_product = jnp.einsum('sjl,sjc->slc', basis_block, even_block)
        odd_product = jnp.einsum('sjl,sjc->slc', basis_block, odd_block)
        parity_odd = (degree[None, :] - group_orders[:, None]) % 2 == 1
        chosen = jnp.where(parity_odd[:, :, None], odd_product, even_product)
        keep_mask = (degree[None, :] >= group_orders[:, None]) & (group_orders >= 0)[:, None]
        return jnp.where(keep_mask[:, :, None], chosen, 0.0).astype(jnp.bfloat16)
    blocks = lax.map(one_group, jnp.arange(slot_all // SLOTS, dtype=jnp.int32))
    return blocks.reshape(slot_all, LDEG, 2 * snap_count)

def reference(fields_grid, basis, order_table, panel_modes):
    snap_count = fields_grid.shape[1]
    orders = order_table.reshape(-1).astype(jnp.int32)
    slot_all = orders.shape[0]
    dft = dft_table(orders, NLON)
    coefficients = lax.map(lambda grid_one: field_coefficients(grid_one, basis, orders, dft), fields_grid)
    mode_order = panel_modes[0].astype(jnp.int32)
    mode_degree = panel_modes[1].astype(jnp.int32)
    slot_of_mode = jnp.argmax(orders[None, :] == mode_order[:, None], axis=1).astype(jnp.int32)
    mode_values = coefficients[:, slot_of_mode, mode_degree, :]
    columns = mode_values.astype(jnp.float32).reshape(2, NMODE * 2, snap_count)
    centered = (columns - lax.optimization_barrier(jnp.mean(columns, axis=2, keepdims=True))).astype(jnp.bfloat16)
    scale = 1.0 / (snap_count - 1)

    def one_field(index):
        own = coefficients[index]
        partner = centered[1 - index]

        def one_group(group):
            start = (group * SLOTS).astype(jnp.int32)
            block = lax.dynamic_slice_in_dim(own, start, SLOTS, 0).reshape(SLOTS * LDEG * 2, snap_count)
            values = jnp.dot(block, partner.T, preferred_element_type=jnp.float32) * scale
            return values.astype(jnp.bfloat16).reshape(SLOTS, 2 * LDEG, 2 * NMODE)
        return lax.map(one_group, jnp.arange(slot_all // SLOTS, dtype=jnp.int32)).reshape(slot_all, 2 * LDEG, 2 * NMODE)
    return lax.map(one_field, jnp.arange(2, dtype=jnp.int32))
```

```python
import functools
import math

import jax
import jax.numpy as jnp
import numpy as np
from jax import lax
from jax.experimental import pallas as pl
from jax.experimental.pallas import tpu as pltpu
from jax.sharding import PartitionSpec as P

BF = jnp.bfloat16
F32 = jnp.float32
NT = (((1,), (1,)), ((), ()))


def iota(shape, dim):
    return lax.broadcasted_iota(jnp.int32, shape, dim)


def mm(a, b):
    return jnp.dot(a, b, preferred_element_type=F32)


def mm_nt(a, b):
    return lax.dot_general(a, b, NT, preferred_element_type=F32)


def kernel(
    lat_count, snap, pairs, lon, slots, degs, per_dev, tail,
    orders_ref, x_ref, basis_ref, table_ref, cols_ref, row_ref,
    out_ref,
    send, recv, mode_send, mode_recv, perm, rows,
    send_sem, recv_sem, mode_send_sem, mode_recv_sem,
):
    me = lax.axis_index("lat")
    field = lax.axis_index("field")
    other = 1 - field
    pair_total = lat_count * pairs
    width = 2 * snap
    block = 2 * slots
    head = pairs * block
    all_rows = lat_count * block
    tail_rows = lat_count * tail
    used = pairs * per_dev

    barrier = pltpu.get_barrier_semaphore()

    def greet_own(k, c):
        pl.semaphore_signal(barrier, inc=1, device_id=(lax.rem(me + k, lat_count), field),
                            device_id_type=pl.DeviceIdType.MESH)
        return c

    def greet_other(k, c):
        pl.semaphore_signal(barrier, inc=1, device_id=(lax.rem(me + k, lat_count), other),
                            device_id_type=pl.DeviceIdType.MESH)
        return c

    lax.fori_loop(1, lat_count, greet_own, 0)
    lax.fori_loop(0, lat_count, greet_other, 0)

    order_col = cols_ref[:, 0:1]
    mode_col = cols_ref[:, 1:2]
    deg_col = cols_ref[:, 2:3]
    nord = table_ref.shape[0] // 2
    parity_row = iota((all_rows, 1), 0) // slots % 2
    want = jnp.where(order_col >= 0, order_col + nord * parity_row, -1)
    onehot = (iota((all_rows, 2 * nord), 1) == want).astype(F32).astype(BF)
    dft = mm(onehot, table_ref[...]).astype(BF)
    rho = iota((tail_rows, 1), 0) % tail
    row_order = row_ref[...]
    row_parity = iota((1, all_rows), 1) // slots % 2
    mode_parity = (deg_col - mode_col) % 2
    match = (mode_col == row_order) & (mode_parity == row_parity)
    tail_acc = jnp.zeros((tail_rows, width), F32)
    zero_x = jnp.zeros((snap, 2 * lon), BF)
    for j in range(pairs):
        xj = x_ref[j]
        both = jnp.concatenate(
            [jnp.concatenate([xj, zero_x], axis=1), jnp.concatenate([zero_x, xj], axis=1)], axis=0
        )
        part = (mm_nt(dft, both) * (1.0 / math.sqrt(lon))).astype(BF)
        send[:, j * block:(j + 1) * block, :] = part.reshape(lat_count, block, width)
        mine = match & (rho // per_dev == j)
        tail_acc = tail_acc + mm(mine.astype(F32).astype(BF), part)
    at_degree = (iota((tail_rows, degs), 1) == deg_col) & (rho >= used) & (rho < used + per_dev)
    basis_acc = jnp.zeros((tail_rows, pair_total), F32)
    for s in range(slots):
        pick = at_degree & (mode_col == orders_ref[me, s])
        basis_acc = basis_acc + mm_nt(pick.astype(F32).astype(BF), basis_ref[s])
    wide = jnp.concatenate(
        [basis_acc, jnp.zeros((tail_rows, width - pair_total), F32)], axis=1
    )
    tail_all = (tail_acc + wide).astype(BF)
    send[:, head:head + tail, :] = tail_all.reshape(lat_count, tail, width)

    pl.semaphore_wait(barrier, 2 * lat_count - 1)

    def block_copy(dst, src):
        return pltpu.make_async_remote_copy(
            src_ref=send.at[dst], dst_ref=recv.at[src],
            send_sem=send_sem.at[dst], recv_sem=recv_sem.at[src],
            device_id=(dst, field), device_id_type=pl.DeviceIdType.MESH,
        )

    def start_block(k, c):
        block_copy(lax.rem(me + k, lat_count), me).start()
        return c

    lax.fori_loop(1, lat_count, start_block, 0)
    recv[me] = send[me]

    k_rows = slots * 2 * pair_total
    for s in range(slots):
        shape = (2 * pair_total, k_rows // 1)
        r = iota((2 * pair_total, 1), 0)
        p = r // pair_total
        j = r % pair_total
        target = j * block + p * slots + s
        perm[s * 2 * pair_total:(s + 1) * 2 * pair_total, :] = (
            iota((2 * pair_total, lat_count * head), 1) == target
        ).astype(F32).astype(BF)
    dup = (iota((2 * degs, degs), 0) // 2 == iota((2 * degs, degs), 1)).astype(F32).astype(BF)
    for s in range(slots):
        order = orders_ref[me, s]
        deg = iota((2 * degs, pair_total), 0) // 2
        base = mm_nt(dup, basis_ref[s])
        keep = (deg >= order) & (order >= 0)
        odd = (deg - order) % 2
        even_part = jnp.where(keep & (odd == 0), base, 0.0)
        odd_part = jnp.where(keep & (odd == 1), base, 0.0)
        rows[s] = jnp.concatenate([even_part, odd_part], axis=1).astype(BF)
    src_of = iota((width, tail_rows), 1) // tail
    rho_of = iota((width, tail_rows), 1) % tail
    spread = (
        (iota((width, tail_rows), 0) == src_of * pairs + rho_of // per_dev) & (rho_of < used)
    ).astype(F32).astype(BF)
    own_row = iota((tail, tail_rows), 0) - used == iota((tail, tail_rows), 1) % tail % per_dev

    def wait_block(k, c):
        src = lax.rem(me + k, lat_count)
        block_copy(src, src).wait_recv()
        return c

    lax.fori_loop(1, lat_count, wait_block, 0)

    tails = recv[:, head:head + tail, :]
    summed = jnp.sum(tails.astype(F32), axis=0).astype(BF)
    weights = jnp.where(own_row, mm(summed, spread), 0.0).astype(BF)
    mode_send[...] = mm(weights, tails.reshape(tail_rows, width)).astype(BF)

    def mode_copy(dst, src):
        return pltpu.make_async_remote_copy(
            src_ref=mode_send, dst_ref=mode_recv.at[src],
            send_sem=mode_send_sem.at[dst], recv_sem=mode_recv_sem.at[src],
            device_id=(dst, other), device_id_type=pl.DeviceIdType.MESH,
        )

    def start_mode(k, c):
        mode_copy(lax.rem(me + k, lat_count), me).start()
        return c

    lax.fori_loop(0, lat_count, start_mode, 0)

    heads = recv[:, 0:head, :].reshape(lat_count * head, width)
    sorted_rows = mm(perm[...], heads).astype(BF)
    same_r = iota((2 * degs, width), 1) // snap == iota((2 * degs, width), 0) % 2
    coefs = []
    for s in range(slots):
        value = mm(rows[s], sorted_rows[s * 2 * pair_total:(s + 1) * 2 * pair_total])
        coefs.append(jnp.where(same_r, value, 0.0).astype(BF))

    modes = lat_count * per_dev
    cu = iota((2 * modes, tail_rows), 0)
    mode_at = cu // 2 // per_dev * tail + used + cu // 2 % per_dev
    expand = (iota((2 * modes, tail_rows), 1) == mode_at).astype(F32).astype(BF)

    def wait_mode(k, c):
        src = lax.rem(me + k, lat_count)
        mode_copy(src, src).wait_recv()
        return c

    lax.fori_loop(0, lat_count, wait_mode, 0)
    values = mode_recv[...].reshape(tail_rows, width)
    columns = mm(expand, values)
    u_match = iota((2 * modes, width), 1) // snap == iota((2 * modes, width), 0) % 2
    masked = jnp.where(u_match, columns, 0.0)
    mean = jnp.sum(masked, axis=1, keepdims=True) * (1.0 / snap)
    centered = jnp.where(u_match, masked - mean, 0.0)
    twice = (centered + pltpu.roll(centered, snap, 1)).astype(BF)
    for s in range(slots):
        out_ref[s] = (mm_nt(coefs[s], twice) * (1.0 / (snap - 1))).astype(BF)

    def finish(k, c):
        dst = lax.rem(me + k, lat_count)
        block_copy(dst, dst).wait_send()
        return c

    def finish_mode(k, c):
        dst = lax.rem(me + k, lat_count)
        mode_copy(dst, dst).wait_send()
        return c

    lax.fori_loop(1, lat_count, finish, 0)
    lax.fori_loop(0, lat_count, finish_mode, 0)


def dft_constant(nord, lon):
    angles = (np.outer(np.arange(nord), np.arange(lon)) % lon) * (2.0 * math.pi / lon)
    cosine, sine = np.cos(angles), -np.sin(angles)
    even = np.concatenate([cosine, cosine, sine, sine], axis=1)
    odd = np.concatenate([cosine, -cosine, sine, -sine], axis=1)
    return np.concatenate([even, odd], axis=0).astype(np.float32).astype(BF)


def fused(lat_count, tail, fields_grid, basis, order_table, panel_modes):
    _, snap, _, pairs, lon = fields_grid.shape
    slots, pair_total, degs = basis.shape
    modes = panel_modes.shape[1]
    per_dev = modes // lat_count
    width = 2 * snap
    block = 2 * slots
    head = pairs * block
    x = fields_grid[0].transpose(2, 0, 1, 3).reshape(pairs, snap, 2 * lon)
    by_row = jnp.broadcast_to(order_table[:, None, :], (lat_count, 2, slots)).reshape(-1)
    padded = jnp.broadcast_to(
        panel_modes.reshape(2, lat_count, 1, per_dev), (2, lat_count, tail // per_dev, per_dev)
    ).reshape(2, -1)
    cols = jnp.concatenate([by_row[None], padded], axis=0).T
    table = jnp.asarray(dft_constant(degs, lon))
    vmem = pl.BlockSpec(memory_space=pltpu.VMEM)
    body = functools.partial(kernel, lat_count, snap, pairs, lon, slots, degs, per_dev, tail)
    out = pl.pallas_call(
        body,
        out_shape=jax.ShapeDtypeStruct((slots, 2 * degs, 2 * modes), BF),
        in_specs=[pl.BlockSpec(memory_space=pltpu.SMEM)] + [vmem] * 5,
        out_specs=vmem,
        scratch_shapes=[
            pltpu.VMEM((lat_count, head + tail, width), BF),
            pltpu.VMEM((lat_count, head + tail, width), BF),
            pltpu.VMEM((tail, width), BF),
            pltpu.VMEM((lat_count, tail, width), BF),
            pltpu.VMEM((slots * 2 * pair_total, lat_count * head), BF),
            pltpu.VMEM((slots, 2 * degs, 2 * pair_total), BF),
            pltpu.SemaphoreType.DMA((lat_count,)),
            pltpu.SemaphoreType.DMA((lat_count,)),
            pltpu.SemaphoreType.DMA((lat_count,)),
            pltpu.SemaphoreType.DMA((lat_count,)),
        ],
        compiler_params=pltpu.CompilerParams(
            collective_id=0, has_side_effects=True, vmem_limit_bytes=48 * 1024 * 1024
        ),
    )(order_table, x, basis, table, cols, by_row[None])
    return out[None]


def dft_table(orders, lon_count):
    valid_slot = orders >= 0
    safe_orders = jnp.maximum(orders, 0)
    products = lax.broadcasted_iota(jnp.int32, (lon_count, 1), 0) * safe_orders[None, :] % lon_count
    angles = products.astype(jnp.float32) * (2.0 * math.pi / lon_count)
    cosine = jnp.where(valid_slot[None, :], jnp.cos(angles), 0.0).astype(jnp.bfloat16)
    sine_table = jnp.where(valid_slot[None, :], -jnp.sin(angles), 0.0).astype(jnp.bfloat16)
    return jnp.stack([cosine, sine_table], axis=1)


def local(fields_grid, basis, order_table, panel_modes):
    grid_one = fields_grid[0]
    snap_count = grid_one.shape[0]
    pair_count = grid_one.shape[2]
    lon_count = grid_one.shape[3]
    slot_count = order_table.shape[1]
    deg_count = basis.shape[2]
    pair_total = basis.shape[1]
    mode_count = panel_modes.shape[1]
    orders = order_table.reshape(-1)
    slot_all = orders.shape[0]
    dft = dft_table(orders, lon_count)
    fourier = jnp.einsum("thjn,nrk->hkjrt", grid_one, dft, preferred_element_type=jnp.float32) * (
        1.0 / math.sqrt(lon_count)
    )
    fourier = fourier.reshape(2, slot_all, pair_count, 2 * snap_count)
    parity_parts = jnp.stack([fourier[0] + fourier[1], fourier[0] - fourier[1]]).astype(
        jnp.bfloat16
    )
    group_index = lax.axis_index("lat")
    my_orders = lax.dynamic_slice_in_dim(order_table, group_index, 1, 0)[0]
    my_odd = my_orders % 2 == 1
    basis_split = basis.reshape(slot_count, pair_total, deg_count // 2, 2)
    even_rows = basis_split[:, :, :, 0]
    odd_rows = basis_split[:, :, :, 1]
    degree = lax.broadcasted_iota(jnp.int32, (1, deg_count), 1)
    keep_mask = (degree >= my_orders[:, None]) & (my_orders >= 0)[:, None]
    received = lax.all_to_all(parity_parts, "lat", split_axis=1, concat_axis=2, tiled=True)
    first_parity = jnp.where(my_odd[:, None, None], received[1], received[0])
    second = jnp.where(my_odd[:, None, None], received[0], received[1])
    low_degrees = jnp.einsum(
        "sjh,sjc->shc", even_rows, first_parity, preferred_element_type=jnp.float32
    )
    high_degrees = jnp.einsum("sjh,sjc->shc", odd_rows, second, preferred_element_type=jnp.float32)
    joined = jnp.stack([low_degrees, high_degrees], axis=2).reshape(slot_count, deg_count, -1)
    coefficients = jnp.where(keep_mask[:, :, None], joined, 0.0).astype(jnp.bfloat16)
    mode_order = panel_modes[0]
    mode_degree = panel_modes[1]
    onehot = (my_orders[None, :] == mode_order[:, None]).astype(jnp.bfloat16)
    picked = jnp.take(coefficients, mode_degree, axis=1)
    local_values = jnp.einsum("ms,smc->mc", onehot, picked, preferred_element_type=jnp.float32)
    field_index = lax.axis_index("field")
    both_fields = jnp.stack(
        [
            jnp.where(field_index == 0, local_values, 0.0),
            jnp.where(field_index == 1, local_values, 0.0),
        ]
    )
    summed = lax.psum(both_fields, ("lat", "field"))
    other_field = jnp.where(field_index == 0, summed[1], summed[0]).astype(jnp.bfloat16)
    columns = other_field.astype(jnp.float32).reshape(mode_count * 2, snap_count)
    centered = (columns - jnp.mean(columns, axis=1, keepdims=True)).astype(jnp.bfloat16)
    coef_rows = coefficients.reshape(slot_count * deg_count * 2, snap_count)
    panel_values = lax.dot_general(
        coef_rows, centered, (((1,), (1,)), ((), ())), preferred_element_type=jnp.float32
    )
    panel_values = panel_values * (1.0 / (snap_count - 1))
    return panel_values.astype(jnp.bfloat16).reshape(1, slot_count, 2 * deg_count, 2 * mode_count)


def device_program(lat_count, fields_grid, basis, order_table, panel_modes):
    pairs, snap = fields_grid.shape[3], fields_grid.shape[1]
    slots, pair_total, _ = basis.shape
    modes = panel_modes.shape[1]
    per_dev = modes // lat_count
    tail = (pairs + 1) * per_dev if per_dev else 0
    rows = slots * 2 * pair_total
    fits = (
        modes % lat_count == 0
        and tail == 2 * slots
        and tail % 16 == 0
        and 2 * snap == 128
        and pair_total <= 2 * snap
        and rows * rows * 2 <= 8 * 1024 * 1024
    )
    if fits:
        return fused(lat_count, tail, fields_grid, basis, order_table, panel_modes)
    return local(fields_grid, basis, order_table, panel_modes)


def solution(mesh):
    placed = (P("field", None, None, "lat", None), P("lat", None, None), P(), P())
    return jax.shard_map(
        functools.partial(device_program, mesh.shape["lat"]),
        mesh=mesh, in_specs=placed, out_specs=P("field", "lat", None, None), check_vma=False,
    )
```

```python
import functools
import math

import jax
import jax.numpy as jnp
import numpy as np
from jax import lax
from jax.experimental import pallas as pl
from jax.experimental.pallas import tpu as pltpu
from jax.sharding import PartitionSpec as P

BF = jnp.bfloat16
F32 = jnp.float32
NT = (((1,), (1,)), ((), ()))


def iota(shape, dim):
    return lax.broadcasted_iota(jnp.int32, shape, dim)


def mm(a, b):
    return jnp.dot(a, b, preferred_element_type=F32)


def mm_nt(a, b):
    return lax.dot_general(a, b, NT, preferred_element_type=F32)


def kernel(
    lat_count, snap, pairs, lon, slots, degs, per_dev, tail,
    x_hbm, basis_hbm, table_hbm, orders_hbm, modes_hbm,
    out_ref,
    x_ref, basis_ref, table_ref, orders_ref, modes_ref, load_sem,
    send, recv, mode_send, mode_recv, perm, rows,
    send_sem, recv_sem, mode_send_sem, mode_recv_sem,
):
    me = lax.axis_index("lat")
    field = lax.axis_index("field")
    other = 1 - field
    pair_total = lat_count * pairs
    width = 2 * snap
    block = 2 * slots
    head = pairs * block
    all_rows = lat_count * block
    tail_rows = lat_count * tail
    used = pairs * per_dev

    loads = [
        pltpu.make_async_copy(src, dst, load_sem.at[at])
        for at, (src, dst) in enumerate([
            (orders_hbm, orders_ref), (modes_hbm, modes_ref), (table_hbm, table_ref),
            (x_hbm, x_ref), (basis_hbm, basis_ref),
        ])
    ]
    for load in loads:
        load.start()

    barrier = pltpu.get_barrier_semaphore()

    def greet_own(k, c):
        pl.semaphore_signal(barrier, inc=1, device_id=(lax.rem(me + k, lat_count), field),
                            device_id_type=pl.DeviceIdType.MESH)
        return c

    def greet_other(k, c):
        pl.semaphore_signal(barrier, inc=1, device_id=(lax.rem(me + k, lat_count), other),
                            device_id_type=pl.DeviceIdType.MESH)
        return c

    lax.fori_loop(1, lat_count, greet_own, 0)
    lax.fori_loop(0, lat_count, greet_other, 0)

    nord = table_ref.shape[0] // 2
    loads[0].wait()
    loads[1].wait()
    by_slot = orders_ref[...]
    tiled = jnp.concatenate([by_slot] * (2 * lat_count), axis=0)
    here = iota((all_rows, lat_count), 1) == iota((all_rows, lat_count), 0) // block
    order_col = jnp.sum(jnp.where(here, tiled, 0), axis=1, keepdims=True)
    mode_total = lat_count * per_dev
    mode_row = iota((tail_rows, mode_total), 0)
    mode_here = iota((tail_rows, mode_total), 1) == mode_row // tail * per_dev + mode_row % per_dev
    mode_col = jnp.sum(jnp.where(mode_here, modes_ref[0:1, :], 0), axis=1, keepdims=True)
    deg_col = jnp.sum(jnp.where(mode_here, modes_ref[1:2, :], 0), axis=1, keepdims=True)
    my_orders = jnp.sum(
        jnp.where(iota((slots, lat_count), 1) == me, by_slot, 0), axis=1, keepdims=True
    )
    group_of = (iota((lat_count, all_rows), 1) // block == iota((lat_count, all_rows), 0))
    by_lane = mm(by_slot.astype(F32).astype(BF), group_of.astype(F32).astype(BF))
    slot_of = iota((slots, all_rows), 1) % slots == iota((slots, all_rows), 0)
    row_order = jnp.sum(jnp.where(slot_of, by_lane, 0.0), axis=0, keepdims=True).astype(jnp.int32)
    parity_row = iota((all_rows, 1), 0) // slots % 2
    want = jnp.where(order_col >= 0, order_col + nord * parity_row, -1)
    onehot = (iota((all_rows, 2 * nord), 1) == want).astype(F32).astype(BF)
    loads[2].wait()
    dft = mm(onehot, table_ref[...]).astype(BF)
    rho = iota((tail_rows, 1), 0) % tail
    row_parity = iota((1, all_rows), 1) // slots % 2
    mode_parity = (deg_col - mode_col) % 2
    match = (mode_col == row_order) & (mode_parity == row_parity)
    tail_acc = jnp.zeros((tail_rows, width), F32)
    zero_x = jnp.zeros((snap, 2 * lon), BF)
    loads[3].wait()
    for j in range(pairs):
        xj = jnp.concatenate([x_ref[:, j, 0, :], x_ref[:, j, 1, :]], axis=1)
        both = jnp.concatenate(
            [jnp.concatenate([xj, zero_x], axis=1), jnp.concatenate([zero_x, xj], axis=1)], axis=0
        )
        part = (mm_nt(dft, both) * (1.0 / math.sqrt(lon))).astype(BF)
        send[:, j * block:(j + 1) * block, :] = part.reshape(lat_count, block, width)
        mine = match & (rho // per_dev == j)
        tail_acc = tail_acc + mm(mine.astype(F32).astype(BF), part)
    at_degree = (iota((tail_rows, degs), 1) == deg_col) & (rho >= used) & (rho < used + per_dev)
    loads[4].wait()
    basis_acc = jnp.zeros((tail_rows, pair_total), F32)
    for s in range(slots):
        pick = at_degree & (mode_col == my_orders[s:s + 1, :])
        basis_acc = basis_acc + mm_nt(pick.astype(F32).astype(BF), basis_ref[s])
    wide = jnp.concatenate(
        [basis_acc, jnp.zeros((tail_rows, width - pair_total), F32)], axis=1
    )
    tail_all = (tail_acc + wide).astype(BF)
    send[:, head:head + tail, :] = tail_all.reshape(lat_count, tail, width)

    pl.semaphore_wait(barrier, 2 * lat_count - 1)

    def block_copy(dst, src):
        return pltpu.make_async_remote_copy(
            src_ref=send.at[dst], dst_ref=recv.at[src],
            send_sem=send_sem.at[dst], recv_sem=recv_sem.at[src],
            device_id=(dst, field), device_id_type=pl.DeviceIdType.MESH,
        )

    def start_block(k, c):
        block_copy(lax.rem(me + k, lat_count), me).start()
        return c

    lax.fori_loop(1, lat_count, start_block, 0)
    recv[me] = send[me]

    k_rows = slots * 2 * pair_total
    for s in range(slots):
        shape = (2 * pair_total, k_rows // 1)
        r = iota((2 * pair_total, 1), 0)
        p = r // pair_total
        j = r % pair_total
        target = j * block + p * slots + s
        perm[s * 2 * pair_total:(s + 1) * 2 * pair_total, :] = (
            iota((2 * pair_total, lat_count * head), 1) == target
        ).astype(F32).astype(BF)
    dup = (iota((2 * degs, degs), 0) // 2 == iota((2 * degs, degs), 1)).astype(F32).astype(BF)
    for s in range(slots):
        order = my_orders[s:s + 1, :]
        deg = iota((2 * degs, pair_total), 0) // 2
        base = mm_nt(dup, basis_ref[s])
        keep = (deg >= order) & (order >= 0)
        odd = (deg - order) % 2
        even_part = jnp.where(keep & (odd == 0), base, 0.0)
        odd_part = jnp.where(keep & (odd == 1), base, 0.0)
        rows[s] = jnp.concatenate([even_part, odd_part], axis=1).astype(BF)
    src_of = iota((width, tail_rows), 1) // tail
    rho_of = iota((width, tail_rows), 1) % tail
    spread = (
        (iota((width, tail_rows), 0) == src_of * pairs + rho_of // per_dev) & (rho_of < used)
    ).astype(F32).astype(BF)
    own_row = iota((tail, tail_rows), 0) - used == iota((tail, tail_rows), 1) % tail % per_dev

    def wait_block(k, c):
        src = lax.rem(me + k, lat_count)
        block_copy(src, src).wait_recv()
        return c

    lax.fori_loop(1, lat_count, wait_block, 0)

    tails = recv[:, head:head + tail, :]
    summed = jnp.sum(tails.astype(F32), axis=0).astype(BF)
    weights = jnp.where(own_row, mm(summed, spread), 0.0).astype(BF)
    mode_send[...] = mm(weights, tails.reshape(tail_rows, width)).astype(BF)

    def mode_copy(dst, src):
        return pltpu.make_async_remote_copy(
            src_ref=mode_send, dst_ref=mode_recv.at[src],
            send_sem=mode_send_sem.at[dst], recv_sem=mode_recv_sem.at[src],
            device_id=(dst, other), device_id_type=pl.DeviceIdType.MESH,
        )

    def start_mode(k, c):
        mode_copy(lax.rem(me + k, lat_count), me).start()
        return c

    lax.fori_loop(0, lat_count, start_mode, 0)

    heads = recv[:, 0:head, :].reshape(lat_count * head, width)
    sorted_rows = mm(perm[...], heads).astype(BF)
    same_r = iota((2 * degs, width), 1) // snap == iota((2 * degs, width), 0) % 2
    coefs = []
    for s in range(slots):
        value = mm(rows[s], sorted_rows[s * 2 * pair_total:(s + 1) * 2 * pair_total])
        coefs.append(jnp.where(same_r, value, 0.0).astype(BF))

    modes = lat_count * per_dev
    cu = iota((2 * modes, tail_rows), 0)
    mode_at = cu // 2 // per_dev * tail + used + cu // 2 % per_dev
    expand = (iota((2 * modes, tail_rows), 1) == mode_at).astype(F32).astype(BF)

    def wait_mode(k, c):
        src = lax.rem(me + k, lat_count)
        mode_copy(src, src).wait_recv()
        return c

    lax.fori_loop(0, lat_count, wait_mode, 0)
    values = mode_recv[...].reshape(tail_rows, width)
    columns = mm(expand, values)
    u_match = iota((2 * modes, width), 1) // snap == iota((2 * modes, width), 0) % 2
    masked = jnp.where(u_match, columns, 0.0)
    mean = jnp.sum(masked, axis=1, keepdims=True) * (1.0 / snap)
    centered = jnp.where(u_match, masked - mean, 0.0)
    twice = (centered + pltpu.roll(centered, snap, 1)).astype(BF)
    for s in range(slots):
        out_ref[s] = (mm_nt(coefs[s], twice) * (1.0 / (snap - 1))).astype(BF)

    def finish(k, c):
        dst = lax.rem(me + k, lat_count)
        block_copy(dst, dst).wait_send()
        return c

    def finish_mode(k, c):
        dst = lax.rem(me + k, lat_count)
        mode_copy(dst, dst).wait_send()
        return c

    lax.fori_loop(1, lat_count, finish, 0)
    lax.fori_loop(0, lat_count, finish_mode, 0)


def dft_constant(nord, lon):
    angles = (np.outer(np.arange(nord), np.arange(lon)) % lon) * (2.0 * math.pi / lon)
    cosine, sine = np.cos(angles), -np.sin(angles)
    even = np.concatenate([cosine, cosine, sine, sine], axis=1)
    odd = np.concatenate([cosine, -cosine, sine, -sine], axis=1)
    return np.concatenate([even, odd], axis=0).astype(np.float32).astype(BF)


def fused(lat_count, tail, fields_grid, basis, order_table, panel_modes):
    _, snap, _, pairs, lon = fields_grid.shape
    slots, pair_total, degs = basis.shape
    modes = panel_modes.shape[1]
    per_dev = modes // lat_count
    width = 2 * snap
    block = 2 * slots
    head = pairs * block
    x = fields_grid[0].transpose(0, 2, 1, 3)
    table = jnp.asarray(dft_constant(degs, lon))
    vmem = pl.BlockSpec(memory_space=pltpu.VMEM)
    body = functools.partial(kernel, lat_count, snap, pairs, lon, slots, degs, per_dev, tail)
    out = pl.pallas_call(
        body,
        out_shape=jax.ShapeDtypeStruct((slots, 2 * degs, 2 * modes), BF),
        in_specs=[pl.BlockSpec(memory_space=pl.ANY)] * 5,
        out_specs=vmem,
        scratch_shapes=[
            pltpu.VMEM(x.shape, BF),
            pltpu.VMEM(basis.shape, BF),
            pltpu.VMEM(table.shape, BF),
            pltpu.VMEM((slots, lat_count), jnp.int32),
            pltpu.VMEM(panel_modes.shape, jnp.int32),
            pltpu.SemaphoreType.DMA((5,)),
            pltpu.VMEM((lat_count, head + tail, width), BF),
            pltpu.VMEM((lat_count, head + tail, width), BF),
            pltpu.VMEM((tail, width), BF),
            pltpu.VMEM((lat_count, tail, width), BF),
            pltpu.VMEM((slots * 2 * pair_total, lat_count * head), BF),
            pltpu.VMEM((slots, 2 * degs, 2 * pair_total), BF),
            pltpu.SemaphoreType.DMA((lat_count,)),
            pltpu.SemaphoreType.DMA((lat_count,)),
            pltpu.SemaphoreType.DMA((lat_count,)),
            pltpu.SemaphoreType.DMA((lat_count,)),
        ],
        compiler_params=pltpu.CompilerParams(
            collective_id=0, has_side_effects=True, vmem_limit_bytes=63 * 1024 * 1024
        ),
    )(x, basis, table, order_table.T, panel_modes)
    return out[None]


def dft_table(orders, lon_count):
    valid_slot = orders >= 0
    safe_orders = jnp.maximum(orders, 0)
    products = lax.broadcasted_iota(jnp.int32, (lon_count, 1), 0) * safe_orders[None, :] % lon_count
    angles = products.astype(jnp.float32) * (2.0 * math.pi / lon_count)
    cosine = jnp.where(valid_slot[None, :], jnp.cos(angles), 0.0).astype(jnp.bfloat16)
    sine_table = jnp.where(valid_slot[None, :], -jnp.sin(angles), 0.0).astype(jnp.bfloat16)
    return jnp.stack([cosine, sine_table], axis=1)


def local(fields_grid, basis, order_table, panel_modes):
    grid_one = fields_grid[0]
    snap_count = grid_one.shape[0]
    pair_count = grid_one.shape[2]
    lon_count = grid_one.shape[3]
    slot_count = order_table.shape[1]
    deg_count = basis.shape[2]
    pair_total = basis.shape[1]
    mode_count = panel_modes.shape[1]
    orders = order_table.reshape(-1)
    slot_all = orders.shape[0]
    dft = dft_table(orders, lon_count)
    fourier = jnp.einsum("thjn,nrk->hkjrt", grid_one, dft, preferred_element_type=jnp.float32) * (
        1.0 / math.sqrt(lon_count)
    )
    fourier = fourier.reshape(2, slot_all, pair_count, 2 * snap_count)
    parity_parts = jnp.stack([fourier[0] + fourier[1], fourier[0] - fourier[1]]).astype(
        jnp.bfloat16
    )
    group_index = lax.axis_index("lat")
    my_orders = lax.dynamic_slice_in_dim(order_table, group_index, 1, 0)[0]
    my_odd = my_orders % 2 == 1
    basis_split = basis.reshape(slot_count, pair_total, deg_count // 2, 2)
    even_rows = basis_split[:, :, :, 0]
    odd_rows = basis_split[:, :, :, 1]
    degree = lax.broadcasted_iota(jnp.int32, (1, deg_count), 1)
    keep_mask = (degree >= my_orders[:, None]) & (my_orders >= 0)[:, None]
    received = lax.all_to_all(parity_parts, "lat", split_axis=1, concat_axis=2, tiled=True)
    first_parity = jnp.where(my_odd[:, None, None], received[1], received[0])
    second = jnp.where(my_odd[:, None, None], received[0], received[1])
    low_degrees = jnp.einsum(
        "sjh,sjc->shc", even_rows, first_parity, preferred_element_type=jnp.float32
    )
    high_degrees = jnp.einsum("sjh,sjc->shc", odd_rows, second, preferred_element_type=jnp.float32)
    joined = jnp.stack([low_degrees, high_degrees], axis=2).reshape(slot_count, deg_count, -1)
    coefficients = jnp.where(keep_mask[:, :, None], joined, 0.0).astype(jnp.bfloat16)
    mode_order = panel_modes[0]
    mode_degree = panel_modes[1]
    onehot = (my_orders[None, :] == mode_order[:, None]).astype(jnp.bfloat16)
    picked = jnp.take(coefficients, mode_degree, axis=1)
    local_values = jnp.einsum("ms,smc->mc", onehot, picked, preferred_element_type=jnp.float32)
    field_index = lax.axis_index("field")
    both_fields = jnp.stack(
        [
            jnp.where(field_index == 0, local_values, 0.0),
            jnp.where(field_index == 1, local_values, 0.0),
        ]
    )
    summed = lax.psum(both_fields, ("lat", "field"))
    other_field = jnp.where(field_index == 0, summed[1], summed[0]).astype(jnp.bfloat16)
    columns = other_field.astype(jnp.float32).reshape(mode_count * 2, snap_count)
    centered = (columns - jnp.mean(columns, axis=1, keepdims=True)).astype(jnp.bfloat16)
    coef_rows = coefficients.reshape(slot_count * deg_count * 2, snap_count)
    panel_values = lax.dot_general(
        coef_rows, centered, (((1,), (1,)), ((), ())), preferred_element_type=jnp.float32
    )
    panel_values = panel_values * (1.0 / (snap_count - 1))
    return panel_values.astype(jnp.bfloat16).reshape(1, slot_count, 2 * deg_count, 2 * mode_count)


def device_program(lat_count, fields_grid, basis, order_table, panel_modes):
    pairs, snap = fields_grid.shape[3], fields_grid.shape[1]
    slots, pair_total, _ = basis.shape
    modes = panel_modes.shape[1]
    per_dev = modes // lat_count
    tail = (pairs + 1) * per_dev if per_dev else 0
    rows = slots * 2 * pair_total
    fits = (
        modes % lat_count == 0
        and tail == 2 * slots
        and tail % 16 == 0
        and 2 * snap == 128
        and slots == 8
        and basis.shape[2] <= 256
        and pair_total <= 2 * snap
        and rows * rows * 2 <= 8 * 1024 * 1024
    )
    if fits:
        return fused(lat_count, tail, fields_grid, basis, order_table, panel_modes)
    return local(fields_grid, basis, order_table, panel_modes)


def solution(mesh):
    placed = (P("field", None, None, "lat", None), P("lat", None, None), P(), P())
    return jax.shard_map(
        functools.partial(device_program, mesh.shape["lat"]),
        mesh=mesh, in_specs=placed, out_specs=P("field", "lat", None, None), check_vma=False,
    )
```

```python
import functools
import math

import jax
import jax.numpy as jnp
import numpy as np
from jax import lax
from jax.experimental import pallas as pl
from jax.experimental.pallas import tpu as pltpu
from jax.sharding import PartitionSpec as P

BF = jnp.bfloat16
F32 = jnp.float32
NT = (((1,), (1,)), ((), ()))


def iota(shape, dim):
    return lax.broadcasted_iota(jnp.int32, shape, dim)


def mm(a, b):
    return jnp.dot(a, b, preferred_element_type=F32)


def mm_nt(a, b):
    return lax.dot_general(a, b, NT, preferred_element_type=F32)


def kernel(
    lat_count, snap, pairs, lon, slots, degs, per_dev, tail,
    x_hbm, basis_hbm, table_hbm, orders_hbm, modes_hbm,
    coef_hbm, twice_ref,
    x_ref, basis_ref, table_ref, orders_ref, modes_ref, load_sem,
    send, recv, tail_send, tail_recv, mode_send, mode_recv, perm, rows, coef, coef_sem,
    send_sem, recv_sem, tail_send_sem, tail_recv_sem, mode_send_sem, mode_recv_sem,
):
    me = lax.axis_index("lat")
    field = lax.axis_index("field")
    other = 1 - field
    pair_total = lat_count * pairs
    width = 2 * snap
    block = 2 * slots
    head = pairs * block
    all_rows = lat_count * block
    tail_rows = lat_count * tail
    used = pairs * per_dev

    loads = [
        pltpu.make_async_copy(src, dst, load_sem.at[at])
        for at, (src, dst) in enumerate([
            (orders_hbm, orders_ref), (modes_hbm, modes_ref), (table_hbm, table_ref),
            (x_hbm, x_ref), (basis_hbm, basis_ref),
        ])
    ]
    for load in loads:
        load.start()

    barrier = pltpu.get_barrier_semaphore()

    def greet_own(k, c):
        pl.semaphore_signal(barrier, inc=1, device_id=(lax.rem(me + k, lat_count), field),
                            device_id_type=pl.DeviceIdType.MESH)
        return c

    def greet_other(k, c):
        pl.semaphore_signal(barrier, inc=1, device_id=(lax.rem(me + k, lat_count), other),
                            device_id_type=pl.DeviceIdType.MESH)
        return c

    lax.fori_loop(1, lat_count, greet_own, 0)
    lax.fori_loop(0, lat_count, greet_other, 0)

    nord = table_ref.shape[0] // 2
    loads[0].wait()
    loads[1].wait()
    by_slot = orders_ref[...]
    tiled = jnp.concatenate([by_slot] * (2 * lat_count), axis=0)
    here = iota((all_rows, lat_count), 1) == iota((all_rows, lat_count), 0) // block
    order_col = jnp.sum(jnp.where(here, tiled, 0), axis=1, keepdims=True)
    mode_total = lat_count * per_dev
    mode_row = iota((tail_rows, mode_total), 0)
    mode_here = iota((tail_rows, mode_total), 1) == mode_row // tail * per_dev + mode_row % per_dev
    mode_col = jnp.sum(jnp.where(mode_here, modes_ref[0:1, :], 0), axis=1, keepdims=True)
    deg_col = jnp.sum(jnp.where(mode_here, modes_ref[1:2, :], 0), axis=1, keepdims=True)
    my_orders = jnp.sum(
        jnp.where(iota((slots, lat_count), 1) == me, by_slot, 0), axis=1, keepdims=True
    )
    group_of = (iota((lat_count, all_rows), 1) // block == iota((lat_count, all_rows), 0))
    by_lane = mm(by_slot.astype(F32).astype(BF), group_of.astype(F32).astype(BF))
    slot_of = iota((slots, all_rows), 1) % slots == iota((slots, all_rows), 0)
    row_order = jnp.sum(jnp.where(slot_of, by_lane, 0.0), axis=0, keepdims=True).astype(jnp.int32)
    parity_row = iota((all_rows, 1), 0) // slots % 2
    want = jnp.where(order_col >= 0, order_col + nord * parity_row, -1)
    onehot = (iota((all_rows, 2 * nord), 1) == want).astype(F32).astype(BF)
    loads[2].wait()
    dft = mm(onehot, table_ref[...]).astype(BF)
    rho = iota((tail_rows, 1), 0) % tail
    row_parity = iota((1, all_rows), 1) // slots % 2
    mode_parity = (deg_col - mode_col) % 2
    match = (mode_col == row_order) & (mode_parity == row_parity)
    tail_acc = jnp.zeros((tail_rows, width), F32)
    zero_x = jnp.zeros((snap, 2 * lon), BF)
    loads[3].wait()
    for j in range(pairs):
        xj = jnp.concatenate([x_ref[:, j, 0, :], x_ref[:, j, 1, :]], axis=1)
        both = jnp.concatenate(
            [jnp.concatenate([xj, zero_x], axis=1), jnp.concatenate([zero_x, xj], axis=1)], axis=0
        )
        part = (mm_nt(dft, both) * (1.0 / math.sqrt(lon))).astype(BF)
        send[:, j * block:(j + 1) * block, :] = part.reshape(lat_count, block, width)
        mine = match & (rho // per_dev == j)
        tail_acc = tail_acc + mm(mine.astype(F32).astype(BF), part)
    at_degree = (iota((tail_rows, degs), 1) == deg_col) & (rho >= used) & (rho < used + per_dev)
    loads[4].wait()
    basis_acc = jnp.zeros((tail_rows, pair_total), F32)
    for s in range(slots):
        pick = at_degree & (mode_col == my_orders[s:s + 1, :])
        basis_acc = basis_acc + mm_nt(pick.astype(F32).astype(BF), basis_ref[s])
    wide = jnp.concatenate(
        [basis_acc, jnp.zeros((tail_rows, width - pair_total), F32)], axis=1
    )
    tail_all = (tail_acc + wide).astype(BF)
    tail_send[...] = tail_all.reshape(lat_count, tail, width)

    pl.semaphore_wait(barrier, 2 * lat_count - 1)

    def block_copy(dst, src):
        return pltpu.make_async_remote_copy(
            src_ref=send.at[dst], dst_ref=recv.at[src],
            send_sem=send_sem.at[dst], recv_sem=recv_sem.at[src],
            device_id=(dst, field), device_id_type=pl.DeviceIdType.MESH,
        )

    def tail_copy(dst, src):
        return pltpu.make_async_remote_copy(
            src_ref=tail_send.at[dst], dst_ref=tail_recv.at[src],
            send_sem=tail_send_sem.at[dst], recv_sem=tail_recv_sem.at[src],
            device_id=(dst, field), device_id_type=pl.DeviceIdType.MESH,
        )

    def start_tail(k, c):
        tail_copy(lax.rem(me + k, lat_count), me).start()
        return c

    lax.fori_loop(1, lat_count, start_tail, 0)

    def start_block(k, c):
        block_copy(lax.rem(me + k, lat_count), me).start()
        return c

    lax.fori_loop(1, lat_count, start_block, 0)
    recv[me] = send[me]
    tail_recv[me] = tail_send[me]

    src_of = iota((width, tail_rows), 1) // tail
    rho_of = iota((width, tail_rows), 1) % tail
    spread = (
        (iota((width, tail_rows), 0) == src_of * pairs + rho_of // per_dev) & (rho_of < used)
    ).astype(F32).astype(BF)
    own_row = iota((tail, tail_rows), 0) - used == iota((tail, tail_rows), 1) % tail % per_dev

    k_rows = slots * 2 * pair_total
    for s in range(slots):
        shape = (2 * pair_total, k_rows // 1)
        r = iota((2 * pair_total, 1), 0)
        p = r // pair_total
        j = r % pair_total
        target = j * block + p * slots + s
        perm[s * 2 * pair_total:(s + 1) * 2 * pair_total, :] = (
            iota((2 * pair_total, lat_count * head), 1) == target
        ).astype(F32).astype(BF)
    dup = (iota((2 * degs, degs), 0) // 2 == iota((2 * degs, degs), 1)).astype(F32).astype(BF)
    for s in range(slots):
        order = my_orders[s:s + 1, :]
        deg = iota((2 * degs, pair_total), 0) // 2
        base = mm_nt(dup, basis_ref[s])
        keep = (deg >= order) & (order >= 0)
        odd = (deg - order) % 2
        even_part = jnp.where(keep & (odd == 0), base, 0.0)
        odd_part = jnp.where(keep & (odd == 1), base, 0.0)
        rows[s] = jnp.concatenate([even_part, odd_part], axis=1).astype(BF)
    def wait_tail(k, c):
        src = lax.rem(me + k, lat_count)
        tail_copy(src, src).wait_recv()
        return c

    lax.fori_loop(1, lat_count, wait_tail, 0)

    tails = tail_recv[...]
    summed = jnp.sum(tails.astype(F32), axis=0).astype(BF)
    weights = jnp.where(own_row, mm(summed, spread), 0.0).astype(BF)
    mode_send[...] = mm(weights, tails.reshape(tail_rows, width)).astype(BF)

    def mode_copy(dst, src):
        return pltpu.make_async_remote_copy(
            src_ref=mode_send, dst_ref=mode_recv.at[src],
            send_sem=mode_send_sem.at[dst], recv_sem=mode_recv_sem.at[src],
            device_id=(dst, other), device_id_type=pl.DeviceIdType.MESH,
        )

    def start_mode(k, c):
        mode_copy(lax.rem(me + k, lat_count), me).start()
        return c

    lax.fori_loop(0, lat_count, start_mode, 0)

    def wait_block(k, c):
        src = lax.rem(me + k, lat_count)
        block_copy(src, src).wait_recv()
        return c

    lax.fori_loop(1, lat_count, wait_block, 0)

    heads = recv[...].reshape(lat_count * head, width)
    sorted_rows = mm(perm[...], heads).astype(BF)
    same_r = iota((2 * degs, width), 1) // snap == iota((2 * degs, width), 0) % 2
    for s in range(slots):
        value = mm(rows[s], sorted_rows[s * 2 * pair_total:(s + 1) * 2 * pair_total])
        coef[s] = jnp.where(same_r, value, 0.0).astype(BF)
    coef_out = pltpu.make_async_copy(coef, coef_hbm, coef_sem)
    coef_out.start()

    modes = lat_count * per_dev
    cu = iota((2 * modes, tail_rows), 0)
    mode_at = cu // 2 // per_dev * tail + used + cu // 2 % per_dev
    expand = (iota((2 * modes, tail_rows), 1) == mode_at).astype(F32).astype(BF)

    def wait_mode(k, c):
        src = lax.rem(me + k, lat_count)
        mode_copy(src, src).wait_recv()
        return c

    lax.fori_loop(0, lat_count, wait_mode, 0)
    values = mode_recv[...].reshape(tail_rows, width)
    columns = mm(expand, values)
    u_match = iota((2 * modes, width), 1) // snap == iota((2 * modes, width), 0) % 2
    masked = jnp.where(u_match, columns, 0.0)
    mean = jnp.sum(masked, axis=1, keepdims=True) * (1.0 / snap)
    centered = jnp.where(u_match, masked - mean, 0.0)
    twice_ref[...] = (centered + pltpu.roll(centered, snap, 1)).astype(BF)
    coef_out.wait()

    def finish(k, c):
        dst = lax.rem(me + k, lat_count)
        block_copy(dst, dst).wait_send()
        tail_copy(dst, dst).wait_send()
        return c

    def finish_mode(k, c):
        dst = lax.rem(me + k, lat_count)
        mode_copy(dst, dst).wait_send()
        return c

    lax.fori_loop(1, lat_count, finish, 0)
    lax.fori_loop(0, lat_count, finish_mode, 0)


def dft_constant(nord, lon):
    angles = (np.outer(np.arange(nord), np.arange(lon)) % lon) * (2.0 * math.pi / lon)
    cosine, sine = np.cos(angles), -np.sin(angles)
    even = np.concatenate([cosine, cosine, sine, sine], axis=1)
    odd = np.concatenate([cosine, -cosine, sine, -sine], axis=1)
    return np.concatenate([even, odd], axis=0).astype(np.float32).astype(BF)


def fused(lat_count, tail, fields_grid, basis, order_table, panel_modes):
    _, snap, _, pairs, lon = fields_grid.shape
    slots, pair_total, degs = basis.shape
    modes = panel_modes.shape[1]
    per_dev = modes // lat_count
    width = 2 * snap
    block = 2 * slots
    head = pairs * block
    x = fields_grid[0].transpose(0, 2, 1, 3)
    table = jnp.asarray(dft_constant(degs, lon))
    vmem = pl.BlockSpec(memory_space=pltpu.VMEM)
    body = functools.partial(kernel, lat_count, snap, pairs, lon, slots, degs, per_dev, tail)
    coef, twice = pl.pallas_call(
        body,
        out_shape=(
            jax.ShapeDtypeStruct((slots, 2 * degs, width), BF),
            jax.ShapeDtypeStruct((2 * modes, width), BF),
        ),
        in_specs=[pl.BlockSpec(memory_space=pl.ANY)] * 5,
        out_specs=(pl.BlockSpec(memory_space=pl.ANY), vmem),
        scratch_shapes=[
            pltpu.VMEM(x.shape, BF),
            pltpu.VMEM(basis.shape, BF),
            pltpu.VMEM(table.shape, BF),
            pltpu.VMEM((slots, lat_count), jnp.int32),
            pltpu.VMEM(panel_modes.shape, jnp.int32),
            pltpu.SemaphoreType.DMA((5,)),
            pltpu.VMEM((lat_count, head, width), BF),
            pltpu.VMEM((lat_count, head, width), BF),
            pltpu.VMEM((lat_count, tail, width), BF),
            pltpu.VMEM((lat_count, tail, width), BF),
            pltpu.VMEM((tail, width), BF),
            pltpu.VMEM((lat_count, tail, width), BF),
            pltpu.VMEM((slots * 2 * pair_total, lat_count * head), BF),
            pltpu.VMEM((slots, 2 * degs, 2 * pair_total), BF),
            pltpu.VMEM((slots, 2 * degs, width), BF),
            pltpu.SemaphoreType.DMA,
            pltpu.SemaphoreType.DMA((lat_count,)),
            pltpu.SemaphoreType.DMA((lat_count,)),
            pltpu.SemaphoreType.DMA((lat_count,)),
            pltpu.SemaphoreType.DMA((lat_count,)),
            pltpu.SemaphoreType.DMA((lat_count,)),
            pltpu.SemaphoreType.DMA((lat_count,)),
        ],
        compiler_params=pltpu.CompilerParams(
            collective_id=0, has_side_effects=True, vmem_limit_bytes=63 * 1024 * 1024
        ),
    )(x, basis, table, order_table.T, panel_modes)
    panel = lax.dot_general(
        coef.reshape(slots * 2 * degs, width), twice, NT, preferred_element_type=F32
    ) * (1.0 / (snap - 1))
    return panel.astype(BF).reshape(1, slots, 2 * degs, 2 * modes)


def dft_table(orders, lon_count):
    valid_slot = orders >= 0
    safe_orders = jnp.maximum(orders, 0)
    products = lax.broadcasted_iota(jnp.int32, (lon_count, 1), 0) * safe_orders[None, :] % lon_count
    angles = products.astype(jnp.float32) * (2.0 * math.pi / lon_count)
    cosine = jnp.where(valid_slot[None, :], jnp.cos(angles), 0.0).astype(jnp.bfloat16)
    sine_table = jnp.where(valid_slot[None, :], -jnp.sin(angles), 0.0).astype(jnp.bfloat16)
    return jnp.stack([cosine, sine_table], axis=1)


def local(fields_grid, basis, order_table, panel_modes):
    grid_one = fields_grid[0]
    snap_count = grid_one.shape[0]
    pair_count = grid_one.shape[2]
    lon_count = grid_one.shape[3]
    slot_count = order_table.shape[1]
    deg_count = basis.shape[2]
    pair_total = basis.shape[1]
    mode_count = panel_modes.shape[1]
    orders = order_table.reshape(-1)
    slot_all = orders.shape[0]
    dft = dft_table(orders, lon_count)
    fourier = jnp.einsum("thjn,nrk->hkjrt", grid_one, dft, preferred_element_type=jnp.float32) * (
        1.0 / math.sqrt(lon_count)
    )
    fourier = fourier.reshape(2, slot_all, pair_count, 2 * snap_count)
    parity_parts = jnp.stack([fourier[0] + fourier[1], fourier[0] - fourier[1]]).astype(
        jnp.bfloat16
    )
    group_index = lax.axis_index("lat")
    my_orders = lax.dynamic_slice_in_dim(order_table, group_index, 1, 0)[0]
    my_odd = my_orders % 2 == 1
    basis_split = basis.reshape(slot_count, pair_total, deg_count // 2, 2)
    even_rows = basis_split[:, :, :, 0]
    odd_rows = basis_split[:, :, :, 1]
    degree = lax.broadcasted_iota(jnp.int32, (1, deg_count), 1)
    keep_mask = (degree >= my_orders[:, None]) & (my_orders >= 0)[:, None]
    received = lax.all_to_all(parity_parts, "lat", split_axis=1, concat_axis=2, tiled=True)
    first_parity = jnp.where(my_odd[:, None, None], received[1], received[0])
    second = jnp.where(my_odd[:, None, None], received[0], received[1])
    low_degrees = jnp.einsum(
        "sjh,sjc->shc", even_rows, first_parity, preferred_element_type=jnp.float32
    )
    high_degrees = jnp.einsum("sjh,sjc->shc", odd_rows, second, preferred_element_type=jnp.float32)
    joined = jnp.stack([low_degrees, high_degrees], axis=2).reshape(slot_count, deg_count, -1)
    coefficients = jnp.where(keep_mask[:, :, None], joined, 0.0).astype(jnp.bfloat16)
    mode_order = panel_modes[0]
    mode_degree = panel_modes[1]
    onehot = (my_orders[None, :] == mode_order[:, None]).astype(jnp.bfloat16)
    picked = jnp.take(coefficients, mode_degree, axis=1)
    local_values = jnp.einsum("ms,smc->mc", onehot, picked, preferred_element_type=jnp.float32)
    field_index = lax.axis_index("field")
    both_fields = jnp.stack(
        [
            jnp.where(field_index == 0, local_values, 0.0),
            jnp.where(field_index == 1, local_values, 0.0),
        ]
    )
    summed = lax.psum(both_fields, ("lat", "field"))
    other_field = jnp.where(field_index == 0, summed[1], summed[0]).astype(jnp.bfloat16)
    columns = other_field.astype(jnp.float32).reshape(mode_count * 2, snap_count)
    centered = (columns - jnp.mean(columns, axis=1, keepdims=True)).astype(jnp.bfloat16)
    coef_rows = coefficients.reshape(slot_count * deg_count * 2, snap_count)
    panel_values = lax.dot_general(
        coef_rows, centered, (((1,), (1,)), ((), ())), preferred_element_type=jnp.float32
    )
    panel_values = panel_values * (1.0 / (snap_count - 1))
    return panel_values.astype(jnp.bfloat16).reshape(1, slot_count, 2 * deg_count, 2 * mode_count)


def device_program(lat_count, fields_grid, basis, order_table, panel_modes):
    pairs, snap = fields_grid.shape[3], fields_grid.shape[1]
    slots, pair_total, _ = basis.shape
    modes = panel_modes.shape[1]
    per_dev = modes // lat_count
    tail = (pairs + 1) * per_dev if per_dev else 0
    rows = slots * 2 * pair_total
    fits = (
        modes % lat_count == 0
        and tail == 2 * slots
        and tail % 16 == 0
        and 2 * snap == 128
        and slots == 8
        and basis.shape[2] <= 256
        and pair_total <= 2 * snap
        and rows * rows * 2 <= 8 * 1024 * 1024
    )
    if fits:
        return fused(lat_count, tail, fields_grid, basis, order_table, panel_modes)
    return local(fields_grid, basis, order_table, panel_modes)


def solution(mesh):
    placed = (P("field", None, None, "lat", None), P("lat", None, None), P(), P())
    return jax.shard_map(
        functools.partial(device_program, mesh.shape["lat"]),
        mesh=mesh, in_specs=placed, out_specs=P("field", "lat", None, None), check_vma=False,
    )
```

```python
import functools
import math

import jax
import jax.numpy as jnp
import numpy as np
from jax import lax
from jax.experimental import pallas as pl
from jax.experimental.pallas import tpu as pltpu
from jax.sharding import PartitionSpec as P

BF = jnp.bfloat16
F32 = jnp.float32
NT = (((1,), (1,)), ((), ()))


def iota(shape, dim):
    return lax.broadcasted_iota(jnp.int32, shape, dim)


def mm(a, b):
    return jnp.dot(a, b, preferred_element_type=F32)


def mm_nt(a, b):
    return lax.dot_general(a, b, NT, preferred_element_type=F32)


def kernel(
    lat_count, snap, pairs, lon, slots, degs, per_dev, tail,
    x_hbm, basis_hbm, table_hbm, orders_hbm, modes_hbm,
    coef_hbm, twice_ref,
    x_ref, basis_ref, table_ref, orders_ref, modes_ref, load_sem,
    send, recv, tail_send, tail_recv, mode_send, mode_recv, perm, rows,
    send_sem, recv_sem, tail_send_sem, tail_recv_sem, mode_send_sem, mode_recv_sem,
):
    me = lax.axis_index("lat")
    field = lax.axis_index("field")
    other = 1 - field
    pair_total = lat_count * pairs
    width = 2 * snap
    block = 2 * slots
    head = pairs * block
    all_rows = lat_count * block
    tail_rows = lat_count * tail
    used = pairs * per_dev

    loads = [
        pltpu.make_async_copy(src, dst, load_sem.at[at])
        for at, (src, dst) in enumerate([
            (orders_hbm, orders_ref), (modes_hbm, modes_ref), (table_hbm, table_ref),
            (x_hbm, x_ref), (basis_hbm, basis_ref),
        ])
    ]
    for load in loads:
        load.start()

    barrier = pltpu.get_barrier_semaphore()

    def greet_own(k, c):
        pl.semaphore_signal(barrier, inc=1, device_id=(lax.rem(me + k, lat_count), field),
                            device_id_type=pl.DeviceIdType.MESH)
        return c

    def greet_other(k, c):
        pl.semaphore_signal(barrier, inc=1, device_id=(lax.rem(me + k, lat_count), other),
                            device_id_type=pl.DeviceIdType.MESH)
        return c

    lax.fori_loop(1, lat_count, greet_own, 0)
    lax.fori_loop(0, lat_count, greet_other, 0)

    nord = table_ref.shape[0] // 2
    loads[0].wait()
    loads[1].wait()
    by_slot = orders_ref[...]
    tiled = jnp.concatenate([by_slot] * (2 * lat_count), axis=0)
    here = iota((all_rows, lat_count), 1) == iota((all_rows, lat_count), 0) // block
    order_col = jnp.sum(jnp.where(here, tiled, 0), axis=1, keepdims=True)
    mode_total = lat_count * per_dev
    mode_row = iota((tail_rows, mode_total), 0)
    mode_here = iota((tail_rows, mode_total), 1) == mode_row // tail * per_dev + mode_row % per_dev
    mode_col = jnp.sum(jnp.where(mode_here, modes_ref[0:1, :], 0), axis=1, keepdims=True)
    deg_col = jnp.sum(jnp.where(mode_here, modes_ref[1:2, :], 0), axis=1, keepdims=True)
    my_orders = jnp.sum(
        jnp.where(iota((slots, lat_count), 1) == me, by_slot, 0), axis=1, keepdims=True
    )
    group_of = (iota((lat_count, all_rows), 1) // block == iota((lat_count, all_rows), 0))
    by_lane = mm(by_slot.astype(F32).astype(BF), group_of.astype(F32).astype(BF))
    slot_of = iota((slots, all_rows), 1) % slots == iota((slots, all_rows), 0)
    row_order = jnp.sum(jnp.where(slot_of, by_lane, 0.0), axis=0, keepdims=True).astype(jnp.int32)
    parity_row = iota((all_rows, 1), 0) // slots % 2
    want = jnp.where(order_col >= 0, order_col + nord * parity_row, -1)
    onehot = (iota((all_rows, 2 * nord), 1) == want).astype(F32).astype(BF)
    loads[2].wait()
    dft = mm(onehot, table_ref[...]).astype(BF)
    rho = iota((tail_rows, 1), 0) % tail
    row_parity = iota((1, all_rows), 1) // slots % 2
    mode_parity = (deg_col - mode_col) % 2
    match = (mode_col == row_order) & (mode_parity == row_parity)
    tail_acc = jnp.zeros((tail_rows, width), F32)
    zero_x = jnp.zeros((snap, 2 * lon), BF)
    loads[3].wait()
    for j in range(pairs):
        xj = jnp.concatenate([x_ref[:, j, 0, :], x_ref[:, j, 1, :]], axis=1)
        both = jnp.concatenate(
            [jnp.concatenate([xj, zero_x], axis=1), jnp.concatenate([zero_x, xj], axis=1)], axis=0
        )
        part = (mm_nt(dft, both) * (1.0 / math.sqrt(lon))).astype(BF)
        send[:, j * block:(j + 1) * block, :] = part.reshape(lat_count, block, width)
        mine = match & (rho // per_dev == j)
        tail_acc = tail_acc + mm(mine.astype(F32).astype(BF), part)
    at_degree = (iota((tail_rows, degs), 1) == deg_col) & (rho >= used) & (rho < used + per_dev)
    loads[4].wait()
    basis_acc = jnp.zeros((tail_rows, pair_total), F32)
    for s in range(slots):
        pick = at_degree & (mode_col == my_orders[s:s + 1, :])
        basis_acc = basis_acc + mm_nt(pick.astype(F32).astype(BF), basis_ref[s])
    wide = jnp.concatenate(
        [basis_acc, jnp.zeros((tail_rows, width - pair_total), F32)], axis=1
    )
    tail_all = (tail_acc + wide).astype(BF)
    tail_send[...] = tail_all.reshape(lat_count, tail, width)

    pl.semaphore_wait(barrier, 2 * lat_count - 1)

    def block_copy(dst, src):
        return pltpu.make_async_remote_copy(
            src_ref=send.at[dst], dst_ref=recv.at[src],
            send_sem=send_sem.at[dst], recv_sem=recv_sem.at[src],
            device_id=(dst, field), device_id_type=pl.DeviceIdType.MESH,
        )

    def tail_copy(dst, src):
        return pltpu.make_async_remote_copy(
            src_ref=tail_send.at[dst], dst_ref=tail_recv.at[src],
            send_sem=tail_send_sem.at[dst], recv_sem=tail_recv_sem.at[src],
            device_id=(dst, field), device_id_type=pl.DeviceIdType.MESH,
        )

    def start_tail(k, c):
        tail_copy(lax.rem(me + k, lat_count), me).start()
        return c

    lax.fori_loop(1, lat_count, start_tail, 0)

    def start_block(k, c):
        block_copy(lax.rem(me + k, lat_count), me).start()
        return c

    lax.fori_loop(1, lat_count, start_block, 0)
    recv[me] = send[me]
    tail_recv[me] = tail_send[me]

    src_of = iota((width, tail_rows), 1) // tail
    rho_of = iota((width, tail_rows), 1) % tail
    spread = (
        (iota((width, tail_rows), 0) == src_of * pairs + rho_of // per_dev) & (rho_of < used)
    ).astype(F32).astype(BF)
    own_row = iota((tail, tail_rows), 0) - used == iota((tail, tail_rows), 1) % tail % per_dev

    k_rows = slots * 2 * pair_total
    for s in range(slots):
        shape = (2 * pair_total, k_rows // 1)
        r = iota((2 * pair_total, 1), 0)
        p = r // pair_total
        j = r % pair_total
        target = j * block + p * slots + s
        perm[s * 2 * pair_total:(s + 1) * 2 * pair_total, :] = (
            iota((2 * pair_total, lat_count * head), 1) == target
        ).astype(F32).astype(BF)
    dup = (iota((2 * degs, degs), 0) // 2 == iota((2 * degs, degs), 1)).astype(F32).astype(BF)
    for s in range(slots):
        order = my_orders[s:s + 1, :]
        deg = iota((2 * degs, pair_total), 0) // 2
        base = mm_nt(dup, basis_ref[s])
        keep = (deg >= order) & (order >= 0)
        odd = (deg - order) % 2
        even_part = jnp.where(keep & (odd == 0), base, 0.0)
        odd_part = jnp.where(keep & (odd == 1), base, 0.0)
        rows[s] = jnp.concatenate([even_part, odd_part], axis=1).astype(BF)
    def wait_tail(k, c):
        src = lax.rem(me + k, lat_count)
        tail_copy(src, src).wait_recv()
        return c

    lax.fori_loop(1, lat_count, wait_tail, 0)

    tails = tail_recv[...]
    summed = jnp.sum(tails.astype(F32), axis=0).astype(BF)
    weights = jnp.where(own_row, mm(summed, spread), 0.0).astype(BF)
    mode_send[...] = mm(weights, tails.reshape(tail_rows, width)).astype(BF)

    def mode_copy(dst, src):
        return pltpu.make_async_remote_copy(
            src_ref=mode_send, dst_ref=mode_recv.at[src],
            send_sem=mode_send_sem.at[dst], recv_sem=mode_recv_sem.at[src],
            device_id=(dst, other), device_id_type=pl.DeviceIdType.MESH,
        )

    def start_mode(k, c):
        mode_copy(lax.rem(me + k, lat_count), me).start()
        return c

    lax.fori_loop(0, lat_count, start_mode, 0)

    def wait_block(k, c):
        src = lax.rem(me + k, lat_count)
        block_copy(src, src).wait_recv()
        return c

    lax.fori_loop(1, lat_count, wait_block, 0)

    heads = recv[...].reshape(lat_count * head, width)
    sorted_rows = mm(perm[...], heads).astype(BF)
    same_r = iota((2 * degs, width), 1) // snap == iota((2 * degs, width), 0) % 2
    for s in range(slots):
        value = mm(rows[s], sorted_rows[s * 2 * pair_total:(s + 1) * 2 * pair_total])
        coef_hbm[s] = jnp.where(same_r, value, 0.0).astype(BF)

    modes = lat_count * per_dev
    cu = iota((2 * modes, tail_rows), 0)
    mode_at = cu // 2 // per_dev * tail + used + cu // 2 % per_dev
    expand = (iota((2 * modes, tail_rows), 1) == mode_at).astype(F32).astype(BF)

    def wait_mode(k, c):
        src = lax.rem(me + k, lat_count)
        mode_copy(src, src).wait_recv()
        return c

    lax.fori_loop(0, lat_count, wait_mode, 0)
    values = mode_recv[...].reshape(tail_rows, width)
    columns = mm(expand, values)
    u_match = iota((2 * modes, width), 1) // snap == iota((2 * modes, width), 0) % 2
    masked = jnp.where(u_match, columns, 0.0)
    mean = jnp.sum(masked, axis=1, keepdims=True) * (1.0 / snap)
    centered = jnp.where(u_match, masked - mean, 0.0)
    twice_ref[...] = (centered + pltpu.roll(centered, snap, 1)).astype(BF)

    def finish(k, c):
        dst = lax.rem(me + k, lat_count)
        block_copy(dst, dst).wait_send()
        tail_copy(dst, dst).wait_send()
        return c

    def finish_mode(k, c):
        dst = lax.rem(me + k, lat_count)
        mode_copy(dst, dst).wait_send()
        return c

    lax.fori_loop(1, lat_count, finish, 0)
    lax.fori_loop(0, lat_count, finish_mode, 0)


def dft_constant(nord, lon):
    angles = (np.outer(np.arange(nord), np.arange(lon)) % lon) * (2.0 * math.pi / lon)
    cosine, sine = np.cos(angles), -np.sin(angles)
    even = np.concatenate([cosine, cosine, sine, sine], axis=1)
    odd = np.concatenate([cosine, -cosine, sine, -sine], axis=1)
    return np.concatenate([even, odd], axis=0).astype(np.float32).astype(BF)


def fused(lat_count, tail, fields_grid, basis, order_table, panel_modes):
    _, snap, _, pairs, lon = fields_grid.shape
    slots, pair_total, degs = basis.shape
    modes = panel_modes.shape[1]
    per_dev = modes // lat_count
    width = 2 * snap
    block = 2 * slots
    head = pairs * block
    x = fields_grid[0].transpose(0, 2, 1, 3)
    table = jnp.asarray(dft_constant(degs, lon))
    vmem = pl.BlockSpec(memory_space=pltpu.VMEM)
    body = functools.partial(kernel, lat_count, snap, pairs, lon, slots, degs, per_dev, tail)
    coef, twice = pl.pallas_call(
        body,
        out_shape=(
            jax.ShapeDtypeStruct((slots, 2 * degs, width), BF),
            jax.ShapeDtypeStruct((2 * modes, width), BF),
        ),
        in_specs=[pl.BlockSpec(memory_space=pl.ANY)] * 5,
        out_specs=(vmem, vmem),
        scratch_shapes=[
            pltpu.VMEM(x.shape, BF),
            pltpu.VMEM(basis.shape, BF),
            pltpu.VMEM(table.shape, BF),
            pltpu.VMEM((slots, lat_count), jnp.int32),
            pltpu.VMEM(panel_modes.shape, jnp.int32),
            pltpu.SemaphoreType.DMA((5,)),
            pltpu.VMEM((lat_count, head, width), BF),
            pltpu.VMEM((lat_count, head, width), BF),
            pltpu.VMEM((lat_count, tail, width), BF),
            pltpu.VMEM((lat_count, tail, width), BF),
            pltpu.VMEM((tail, width), BF),
            pltpu.VMEM((lat_count, tail, width), BF),
            pltpu.VMEM((slots * 2 * pair_total, lat_count * head), BF),
            pltpu.VMEM((slots, 2 * degs, 2 * pair_total), BF),
            pltpu.SemaphoreType.DMA((lat_count,)),
            pltpu.SemaphoreType.DMA((lat_count,)),
            pltpu.SemaphoreType.DMA((lat_count,)),
            pltpu.SemaphoreType.DMA((lat_count,)),
            pltpu.SemaphoreType.DMA((lat_count,)),
            pltpu.SemaphoreType.DMA((lat_count,)),
        ],
        compiler_params=pltpu.CompilerParams(
            collective_id=0, has_side_effects=True, vmem_limit_bytes=52 * 1024 * 1024
        ),
    )(*[pltpu.with_memory_space_constraint(v, pltpu.HBM) for v in (x, basis, table, order_table.T, panel_modes)])
    panel = lax.dot_general(
        coef.reshape(slots * 2 * degs, width), twice, NT, preferred_element_type=F32
    ) * (1.0 / (snap - 1))
    return panel.astype(BF).reshape(1, slots, 2 * degs, 2 * modes)


def dft_table(orders, lon_count):
    valid_slot = orders >= 0
    safe_orders = jnp.maximum(orders, 0)
    products = lax.broadcasted_iota(jnp.int32, (lon_count, 1), 0) * safe_orders[None, :] % lon_count
    angles = products.astype(jnp.float32) * (2.0 * math.pi / lon_count)
    cosine = jnp.where(valid_slot[None, :], jnp.cos(angles), 0.0).astype(jnp.bfloat16)
    sine_table = jnp.where(valid_slot[None, :], -jnp.sin(angles), 0.0).astype(jnp.bfloat16)
    return jnp.stack([cosine, sine_table], axis=1)


def local(fields_grid, basis, order_table, panel_modes):
    grid_one = fields_grid[0]
    snap_count = grid_one.shape[0]
    pair_count = grid_one.shape[2]
    lon_count = grid_one.shape[3]
    slot_count = order_table.shape[1]
    deg_count = basis.shape[2]
    pair_total = basis.shape[1]
    mode_count = panel_modes.shape[1]
    orders = order_table.reshape(-1)
    slot_all = orders.shape[0]
    dft = dft_table(orders, lon_count)
    fourier = jnp.einsum("thjn,nrk->hkjrt", grid_one, dft, preferred_element_type=jnp.float32) * (
        1.0 / math.sqrt(lon_count)
    )
    fourier = fourier.reshape(2, slot_all, pair_count, 2 * snap_count)
    parity_parts = jnp.stack([fourier[0] + fourier[1], fourier[0] - fourier[1]]).astype(
        jnp.bfloat16
    )
    group_index = lax.axis_index("lat")
    my_orders = lax.dynamic_slice_in_dim(order_table, group_index, 1, 0)[0]
    my_odd = my_orders % 2 == 1
    basis_split = basis.reshape(slot_count, pair_total, deg_count // 2, 2)
    even_rows = basis_split[:, :, :, 0]
    odd_rows = basis_split[:, :, :, 1]
    degree = lax.broadcasted_iota(jnp.int32, (1, deg_count), 1)
    keep_mask = (degree >= my_orders[:, None]) & (my_orders >= 0)[:, None]
    received = lax.all_to_all(parity_parts, "lat", split_axis=1, concat_axis=2, tiled=True)
    first_parity = jnp.where(my_odd[:, None, None], received[1], received[0])
    second = jnp.where(my_odd[:, None, None], received[0], received[1])
    low_degrees = jnp.einsum(
        "sjh,sjc->shc", even_rows, first_parity, preferred_element_type=jnp.float32
    )
    high_degrees = jnp.einsum("sjh,sjc->shc", odd_rows, second, preferred_element_type=jnp.float32)
    joined = jnp.stack([low_degrees, high_degrees], axis=2).reshape(slot_count, deg_count, -1)
    coefficients = jnp.where(keep_mask[:, :, None], joined, 0.0).astype(jnp.bfloat16)
    mode_order = panel_modes[0]
    mode_degree = panel_modes[1]
    onehot = (my_orders[None, :] == mode_order[:, None]).astype(jnp.bfloat16)
    picked = jnp.take(coefficients, mode_degree, axis=1)
    local_values = jnp.einsum("ms,smc->mc", onehot, picked, preferred_element_type=jnp.float32)
    field_index = lax.axis_index("field")
    both_fields = jnp.stack(
        [
            jnp.where(field_index == 0, local_values, 0.0),
            jnp.where(field_index == 1, local_values, 0.0),
        ]
    )
    summed = lax.psum(both_fields, ("lat", "field"))
    other_field = jnp.where(field_index == 0, summed[1], summed[0]).astype(jnp.bfloat16)
    columns = other_field.astype(jnp.float32).reshape(mode_count * 2, snap_count)
    centered = (columns - jnp.mean(columns, axis=1, keepdims=True)).astype(jnp.bfloat16)
    coef_rows = coefficients.reshape(slot_count * deg_count * 2, snap_count)
    panel_values = lax.dot_general(
        coef_rows, centered, (((1,), (1,)), ((), ())), preferred_element_type=jnp.float32
    )
    panel_values = panel_values * (1.0 / (snap_count - 1))
    return panel_values.astype(jnp.bfloat16).reshape(1, slot_count, 2 * deg_count, 2 * mode_count)


def device_program(lat_count, fields_grid, basis, order_table, panel_modes):
    pairs, snap = fields_grid.shape[3], fields_grid.shape[1]
    slots, pair_total, _ = basis.shape
    modes = panel_modes.shape[1]
    per_dev = modes // lat_count
    tail = (pairs + 1) * per_dev if per_dev else 0
    rows = slots * 2 * pair_total
    fits = (
        modes % lat_count == 0
        and tail == 2 * slots
        and tail % 16 == 0
        and 2 * snap == 128
        and slots == 8
        and basis.shape[2] <= 256
        and pair_total <= 2 * snap
        and rows * rows * 2 <= 8 * 1024 * 1024
    )
    if fits:
        return fused(lat_count, tail, fields_grid, basis, order_table, panel_modes)
    return local(fields_grid, basis, order_table, panel_modes)


def solution(mesh):
    placed = (P("field", None, None, "lat", None), P("lat", None, None), P(), P())
    return jax.shard_map(
        functools.partial(device_program, mesh.shape["lat"]),
        mesh=mesh, in_specs=placed, out_specs=P("field", "lat", None, None), check_vma=False,
    )
```

```python
import functools
import math

import jax
import jax.numpy as jnp
import numpy as np
from jax import lax
from jax.experimental import pallas as pl
from jax.experimental.pallas import tpu as pltpu
from jax.sharding import PartitionSpec as P

BF = jnp.bfloat16
F32 = jnp.float32
NT = (((1,), (1,)), ((), ()))


def iota(shape, dim):
    return lax.broadcasted_iota(jnp.int32, shape, dim)


def mm(a, b):
    return jnp.dot(a, b, preferred_element_type=F32)


def mm_nt(a, b):
    return lax.dot_general(a, b, NT, preferred_element_type=F32)


def kernel(
    lat_count, snap, pairs, lon, slots, degs, per_dev, tail,
    x_hbm, basis_hbm, table_hbm, orders_hbm, modes_hbm,
    coef_hbm, twice_ref,
    x_ref, basis_ref, table_ref, orders_ref, modes_ref, load_sem,
    send, recv, tail_send, tail_recv, mode_send, mode_recv, perm, rows,
    send_sem, recv_sem, tail_send_sem, tail_recv_sem, mode_send_sem, mode_recv_sem,
):
    me = lax.axis_index("lat")
    field = lax.axis_index("field")
    other = 1 - field
    pair_total = lat_count * pairs
    width = 2 * snap
    block = 2 * slots
    head = pairs * block
    all_rows = lat_count * block
    tail_rows = lat_count * tail
    used = pairs * per_dev

    loads = [
        pltpu.make_async_copy(src, dst, load_sem.at[at])
        for at, (src, dst) in enumerate([
            (orders_hbm, orders_ref), (modes_hbm, modes_ref), (table_hbm, table_ref),
            (x_hbm, x_ref), (basis_hbm, basis_ref),
        ])
    ]
    for load in loads:
        load.start()

    barrier = pltpu.get_barrier_semaphore()

    def greet_own(k, c):
        pl.semaphore_signal(barrier, inc=1, device_id=(lax.rem(me + k, lat_count), field),
                            device_id_type=pl.DeviceIdType.MESH)
        return c

    def greet_other(k, c):
        pl.semaphore_signal(barrier, inc=1, device_id=(lax.rem(me + k, lat_count), other),
                            device_id_type=pl.DeviceIdType.MESH)
        return c

    lax.fori_loop(1, lat_count, greet_own, 0)
    lax.fori_loop(0, lat_count, greet_other, 0)

    nord = table_ref.shape[0] // 2
    loads[0].wait()
    loads[1].wait()
    by_slot = orders_ref[...]
    tiled = jnp.concatenate([by_slot] * (2 * lat_count), axis=0)
    here = iota((all_rows, lat_count), 1) == iota((all_rows, lat_count), 0) // block
    order_col = jnp.sum(jnp.where(here, tiled, 0), axis=1, keepdims=True)
    mode_total = lat_count * per_dev
    mode_row = iota((tail_rows, mode_total), 0)
    mode_here = iota((tail_rows, mode_total), 1) == mode_row // tail * per_dev + mode_row % per_dev
    mode_col = jnp.sum(jnp.where(mode_here, modes_ref[0:1, :], 0), axis=1, keepdims=True)
    deg_col = jnp.sum(jnp.where(mode_here, modes_ref[1:2, :], 0), axis=1, keepdims=True)
    my_orders = jnp.sum(
        jnp.where(iota((slots, lat_count), 1) == me, by_slot, 0), axis=1, keepdims=True
    )
    group_of = (iota((lat_count, all_rows), 1) // block == iota((lat_count, all_rows), 0))
    by_lane = mm(by_slot.astype(F32).astype(BF), group_of.astype(F32).astype(BF))
    slot_of = iota((slots, all_rows), 1) % slots == iota((slots, all_rows), 0)
    row_order = jnp.sum(jnp.where(slot_of, by_lane, 0.0), axis=0, keepdims=True).astype(jnp.int32)
    parity_row = iota((all_rows, 1), 0) // slots % 2
    want = jnp.where(order_col >= 0, order_col + nord * parity_row, -1)
    onehot = (iota((all_rows, 2 * nord), 1) == want).astype(F32).astype(BF)
    loads[2].wait()
    dft = mm(onehot, table_ref[...]).astype(BF)
    rho = iota((tail_rows, 1), 0) % tail
    row_parity = iota((1, all_rows), 1) // slots % 2
    mode_parity = (deg_col - mode_col) % 2
    match = (mode_col == row_order) & (mode_parity == row_parity)
    tail_acc = jnp.zeros((tail_rows, width), F32)
    zero_x = jnp.zeros((snap, 2 * lon), BF)
    loads[3].wait()
    for j in range(pairs):
        xj = jnp.concatenate([x_ref[:, j, 0, :], x_ref[:, j, 1, :]], axis=1)
        both = jnp.concatenate(
            [jnp.concatenate([xj, zero_x], axis=1), jnp.concatenate([zero_x, xj], axis=1)], axis=0
        )
        part = (mm_nt(dft, both) * (1.0 / math.sqrt(lon))).astype(BF)
        send[:, j * block:(j + 1) * block, :] = part.reshape(lat_count, block, width)
        mine = match & (rho // per_dev == j)
        tail_acc = tail_acc + mm(mine.astype(F32).astype(BF), part)
    at_degree = (iota((tail_rows, degs), 1) == deg_col) & (rho >= used) & (rho < used + per_dev)
    loads[4].wait()
    basis_acc = jnp.zeros((tail_rows, pair_total), F32)
    for s in range(slots):
        pick = at_degree & (mode_col == my_orders[s:s + 1, :])
        basis_acc = basis_acc + mm_nt(pick.astype(F32).astype(BF), basis_ref[s])
    wide = jnp.concatenate(
        [basis_acc, jnp.zeros((tail_rows, width - pair_total), F32)], axis=1
    )
    tail_all = (tail_acc + wide).astype(BF)
    tail_send[...] = tail_all.reshape(lat_count, tail, width)

    pl.semaphore_wait(barrier, 2 * lat_count - 1)

    def whole(src, dst, count, one_send_sem, one_recv_sem):
        return pltpu.make_async_remote_copy(
            src_ref=src.at[pl.ds(0, count)], dst_ref=dst.at[pl.ds(0, count)],
            send_sem=one_send_sem, recv_sem=one_recv_sem,
            device_id=(me, other), device_id_type=pl.DeviceIdType.MESH,
        )

    def block_copy(dst, src):
        return pltpu.make_async_remote_copy(
            src_ref=send.at[dst], dst_ref=recv.at[src],
            send_sem=send_sem, recv_sem=recv_sem,
            device_id=(dst, field), device_id_type=pl.DeviceIdType.MESH,
        )

    def tail_copy(dst, src):
        return pltpu.make_async_remote_copy(
            src_ref=tail_send.at[dst], dst_ref=tail_recv.at[src],
            send_sem=tail_send_sem, recv_sem=tail_recv_sem,
            device_id=(dst, field), device_id_type=pl.DeviceIdType.MESH,
        )

    def start_tail(k, c):
        tail_copy(lax.rem(me + k, lat_count), me).start()
        return c

    lax.fori_loop(1, lat_count, start_tail, 0)

    def start_block(k, c):
        block_copy(lax.rem(me + k, lat_count), me).start()
        return c

    lax.fori_loop(1, lat_count, start_block, 0)
    recv[me] = send[me]
    tail_recv[me] = tail_send[me]

    src_of = iota((width, tail_rows), 1) // tail
    rho_of = iota((width, tail_rows), 1) % tail
    spread = (
        (iota((width, tail_rows), 0) == src_of * pairs + rho_of // per_dev) & (rho_of < used)
    ).astype(F32).astype(BF)
    own_row = iota((per_dev, tail_rows), 0) == iota((per_dev, tail_rows), 1) % tail % per_dev

    k_rows = slots * 2 * pair_total
    for s in range(slots):
        shape = (2 * pair_total, k_rows // 1)
        r = iota((2 * pair_total, 1), 0)
        p = r // pair_total
        j = r % pair_total
        target = j * block + p * slots + s
        perm[s * 2 * pair_total:(s + 1) * 2 * pair_total, :] = (
            iota((2 * pair_total, lat_count * head), 1) == target
        ).astype(F32).astype(BF)
    dup = (iota((2 * degs, degs), 0) // 2 == iota((2 * degs, degs), 1)).astype(F32).astype(BF)
    for s in range(slots):
        order = my_orders[s:s + 1, :]
        deg = iota((2 * degs, pair_total), 0) // 2
        base = mm_nt(dup, basis_ref[s])
        keep = (deg >= order) & (order >= 0)
        odd = (deg - order) % 2
        even_part = jnp.where(keep & (odd == 0), base, 0.0)
        odd_part = jnp.where(keep & (odd == 1), base, 0.0)
        rows[s] = jnp.concatenate([even_part, odd_part], axis=1).astype(BF)
    all_tails = whole(tail_send, tail_recv, lat_count - 1, tail_send_sem, tail_recv_sem)
    all_tails.wait_recv()

    tails = tail_recv[...]
    summed = jnp.sum(tails.astype(F32), axis=0)[used:used + per_dev].astype(BF)
    weights = jnp.where(own_row, mm(summed, spread), 0.0).astype(BF)
    mode_send[...] = mm(weights, tails.reshape(tail_rows, width)).astype(BF)

    def mode_copy(dst, src):
        return pltpu.make_async_remote_copy(
            src_ref=mode_send, dst_ref=mode_recv.at[src],
            send_sem=mode_send_sem, recv_sem=mode_recv_sem,
            device_id=(dst, other), device_id_type=pl.DeviceIdType.MESH,
        )

    def start_mode(k, c):
        mode_copy(lax.rem(me + k, lat_count), me).start()
        return c

    lax.fori_loop(0, lat_count, start_mode, 0)

    all_blocks = whole(send, recv, lat_count - 1, send_sem, recv_sem)
    all_blocks.wait_recv()

    heads = recv[...].reshape(lat_count * head, width)
    sorted_rows = mm(perm[...], heads).astype(BF)
    same_r = iota((2 * degs, width), 1) // snap == iota((2 * degs, width), 0) % 2
    for s in range(slots):
        value = mm(rows[s], sorted_rows[s * 2 * pair_total:(s + 1) * 2 * pair_total])
        coef_hbm[s] = jnp.where(same_r, value, 0.0).astype(BF)

    modes = lat_count * per_dev
    expand = (iota((2 * modes, modes), 1) == iota((2 * modes, modes), 0) // 2).astype(F32).astype(BF)

    all_modes = whole(mode_recv, mode_recv, lat_count, mode_send_sem, mode_recv_sem)
    all_modes.wait_recv()
    values = mode_recv[...].reshape(modes, width)
    columns = mm(expand, values)
    u_match = iota((2 * modes, width), 1) // snap == iota((2 * modes, width), 0) % 2
    masked = jnp.where(u_match, columns, 0.0)
    mean = jnp.sum(masked, axis=1, keepdims=True) * (1.0 / snap)
    centered = jnp.where(u_match, masked - mean, 0.0)
    twice_ref[...] = (centered + pltpu.roll(centered, snap, 1)).astype(BF)

    all_blocks.wait_send()
    all_tails.wait_send()
    all_modes.wait_send()


def dft_constant(nord, lon):
    angles = (np.outer(np.arange(nord), np.arange(lon)) % lon) * (2.0 * math.pi / lon)
    cosine, sine = np.cos(angles), -np.sin(angles)
    even = np.concatenate([cosine, cosine, sine, sine], axis=1)
    odd = np.concatenate([cosine, -cosine, sine, -sine], axis=1)
    return np.concatenate([even, odd], axis=0).astype(np.float32).astype(BF)


def fused(lat_count, tail, fields_grid, basis, order_table, panel_modes):
    _, snap, _, pairs, lon = fields_grid.shape
    slots, pair_total, degs = basis.shape
    modes = panel_modes.shape[1]
    per_dev = modes // lat_count
    width = 2 * snap
    block = 2 * slots
    head = pairs * block
    x = fields_grid[0].transpose(0, 2, 1, 3)
    table = jnp.asarray(dft_constant(degs, lon))
    vmem = pl.BlockSpec(memory_space=pltpu.VMEM)
    body = functools.partial(kernel, lat_count, snap, pairs, lon, slots, degs, per_dev, tail)
    coef, twice = pl.pallas_call(
        body,
        out_shape=(
            jax.ShapeDtypeStruct((slots, 2 * degs, width), BF),
            jax.ShapeDtypeStruct((2 * modes, width), BF),
        ),
        in_specs=[pl.BlockSpec(memory_space=pl.ANY)] * 5,
        out_specs=(vmem, vmem),
        scratch_shapes=[
            pltpu.VMEM(x.shape, BF),
            pltpu.VMEM(basis.shape, BF),
            pltpu.VMEM(table.shape, BF),
            pltpu.VMEM((slots, lat_count), jnp.int32),
            pltpu.VMEM(panel_modes.shape, jnp.int32),
            pltpu.SemaphoreType.DMA((5,)),
            pltpu.VMEM((lat_count, head, width), BF),
            pltpu.VMEM((lat_count, head, width), BF),
            pltpu.VMEM((lat_count, tail, width), BF),
            pltpu.VMEM((lat_count, tail, width), BF),
            pltpu.VMEM((per_dev, width), BF),
            pltpu.VMEM((lat_count, per_dev, width), BF),
            pltpu.VMEM((slots * 2 * pair_total, lat_count * head), BF),
            pltpu.VMEM((slots, 2 * degs, 2 * pair_total), BF),
            pltpu.SemaphoreType.DMA,
            pltpu.SemaphoreType.DMA,
            pltpu.SemaphoreType.DMA,
            pltpu.SemaphoreType.DMA,
            pltpu.SemaphoreType.DMA,
            pltpu.SemaphoreType.DMA,
        ],
        compiler_params=pltpu.CompilerParams(
            collective_id=0, has_side_effects=True, vmem_limit_bytes=52 * 1024 * 1024
        ),
    )(*[pltpu.with_memory_space_constraint(v, pltpu.HBM) for v in (x, basis, table, order_table.T, panel_modes)])
    panel = lax.dot_general(
        coef.reshape(slots * 2 * degs, width), twice, NT, preferred_element_type=F32
    ) * (1.0 / (snap - 1))
    return panel.astype(BF).reshape(1, slots, 2 * degs, 2 * modes)


def dft_table(orders, lon_count):
    valid_slot = orders >= 0
    safe_orders = jnp.maximum(orders, 0)
    products = lax.broadcasted_iota(jnp.int32, (lon_count, 1), 0) * safe_orders[None, :] % lon_count
    angles = products.astype(jnp.float32) * (2.0 * math.pi / lon_count)
    cosine = jnp.where(valid_slot[None, :], jnp.cos(angles), 0.0).astype(jnp.bfloat16)
    sine_table = jnp.where(valid_slot[None, :], -jnp.sin(angles), 0.0).astype(jnp.bfloat16)
    return jnp.stack([cosine, sine_table], axis=1)


def local(fields_grid, basis, order_table, panel_modes):
    grid_one = fields_grid[0]
    snap_count = grid_one.shape[0]
    pair_count = grid_one.shape[2]
    lon_count = grid_one.shape[3]
    slot_count = order_table.shape[1]
    deg_count = basis.shape[2]
    pair_total = basis.shape[1]
    mode_count = panel_modes.shape[1]
    orders = order_table.reshape(-1)
    slot_all = orders.shape[0]
    dft = dft_table(orders, lon_count)
    fourier = jnp.einsum("thjn,nrk->hkjrt", grid_one, dft, preferred_element_type=jnp.float32) * (
        1.0 / math.sqrt(lon_count)
    )
    fourier = fourier.reshape(2, slot_all, pair_count, 2 * snap_count)
    parity_parts = jnp.stack([fourier[0] + fourier[1], fourier[0] - fourier[1]]).astype(
        jnp.bfloat16
    )
    group_index = lax.axis_index("lat")
    my_orders = lax.dynamic_slice_in_dim(order_table, group_index, 1, 0)[0]
    my_odd = my_orders % 2 == 1
    basis_split = basis.reshape(slot_count, pair_total, deg_count // 2, 2)
    even_rows = basis_split[:, :, :, 0]
    odd_rows = basis_split[:, :, :, 1]
    degree = lax.broadcasted_iota(jnp.int32, (1, deg_count), 1)
    keep_mask = (degree >= my_orders[:, None]) & (my_orders >= 0)[:, None]
    received = lax.all_to_all(parity_parts, "lat", split_axis=1, concat_axis=2, tiled=True)
    first_parity = jnp.where(my_odd[:, None, None], received[1], received[0])
    second = jnp.where(my_odd[:, None, None], received[0], received[1])
    low_degrees = jnp.einsum(
        "sjh,sjc->shc", even_rows, first_parity, preferred_element_type=jnp.float32
    )
    high_degrees = jnp.einsum("sjh,sjc->shc", odd_rows, second, preferred_element_type=jnp.float32)
    joined = jnp.stack([low_degrees, high_degrees], axis=2).reshape(slot_count, deg_count, -1)
    coefficients = jnp.where(keep_mask[:, :, None], joined, 0.0).astype(jnp.bfloat16)
    mode_order = panel_modes[0]
    mode_degree = panel_modes[1]
    onehot = (my_orders[None, :] == mode_order[:, None]).astype(jnp.bfloat16)
    picked = jnp.take(coefficients, mode_degree, axis=1)
    local_values = jnp.einsum("ms,smc->mc", onehot, picked, preferred_element_type=jnp.float32)
    field_index = lax.axis_index("field")
    both_fields = jnp.stack(
        [
            jnp.where(field_index == 0, local_values, 0.0),
            jnp.where(field_index == 1, local_values, 0.0),
        ]
    )
    summed = lax.psum(both_fields, ("lat", "field"))
    other_field = jnp.where(field_index == 0, summed[1], summed[0]).astype(jnp.bfloat16)
    columns = other_field.astype(jnp.float32).reshape(mode_count * 2, snap_count)
    centered = (columns - jnp.mean(columns, axis=1, keepdims=True)).astype(jnp.bfloat16)
    coef_rows = coefficients.reshape(slot_count * deg_count * 2, snap_count)
    panel_values = lax.dot_general(
        coef_rows, centered, (((1,), (1,)), ((), ())), preferred_element_type=jnp.float32
    )
    panel_values = panel_values * (1.0 / (snap_count - 1))
    return panel_values.astype(jnp.bfloat16).reshape(1, slot_count, 2 * deg_count, 2 * mode_count)


def device_program(lat_count, fields_grid, basis, order_table, panel_modes):
    pairs, snap = fields_grid.shape[3], fields_grid.shape[1]
    slots, pair_total, _ = basis.shape
    modes = panel_modes.shape[1]
    per_dev = modes // lat_count
    tail = (pairs + 1) * per_dev if per_dev else 0
    rows = slots * 2 * pair_total
    fits = (
        modes % lat_count == 0
        and tail == 2 * slots
        and tail % 16 == 0
        and 2 * snap == 128
        and slots == 8
        and basis.shape[2] <= 256
        and pair_total <= 2 * snap
        and rows * rows * 2 <= 8 * 1024 * 1024
    )
    if fits:
        return fused(lat_count, tail, fields_grid, basis, order_table, panel_modes)
    return local(fields_grid, basis, order_table, panel_modes)


def solution(mesh):
    placed = (P("field", None, None, "lat", None), P("lat", None, None), P(), P())
    return jax.shard_map(
        functools.partial(device_program, mesh.shape["lat"]),
        mesh=mesh, in_specs=placed, out_specs=P("field", "lat", None, None), check_vma=False,
    )
```

```python
import functools
import math

import jax
import jax.numpy as jnp
import numpy as np
from jax import lax
from jax.experimental import pallas as pl
from jax.experimental.pallas import tpu as pltpu
from jax.sharding import PartitionSpec as P

BF = jnp.bfloat16
F32 = jnp.float32
NT = (((1,), (1,)), ((), ()))


def iota(shape, dim):
    return lax.broadcasted_iota(jnp.int32, shape, dim)


def mm(a, b):
    return jnp.dot(a, b, preferred_element_type=F32)


def mm_nt(a, b):
    return lax.dot_general(a, b, NT, preferred_element_type=F32)


def kernel(
    lat_count, snap, pairs, lon, slots, degs, per_dev, tail,
    x_hbm, basis_hbm, table_hbm, orders_hbm, modes_hbm,
    coef_hbm, twice_ref,
    x_ref, basis_ref, table_ref, orders_ref, modes_ref, load_sem,
    send, recv, tail_send, tail_recv, mode_send, mode_recv, perm, rows,
    send_sem, recv_sem, tail_send_sem, tail_recv_sem, mode_send_sem, mode_recv_sem,
):
    me = lax.axis_index("lat")
    field = lax.axis_index("field")
    other = 1 - field
    pair_total = lat_count * pairs
    width = 2 * snap
    block = 2 * slots
    head = pairs * block
    all_rows = lat_count * block
    tail_rows = lat_count * tail
    used = pairs * per_dev

    loads = [
        pltpu.make_async_copy(src, dst, load_sem.at[at])
        for at, (src, dst) in enumerate([
            (orders_hbm, orders_ref), (modes_hbm, modes_ref), (table_hbm, table_ref),
            (x_hbm, x_ref), (basis_hbm, basis_ref),
        ])
    ]
    for load in loads:
        load.start()

    barrier = pltpu.get_barrier_semaphore()

    def greet_own(k, c):
        pl.semaphore_signal(barrier, inc=1, device_id=(lax.rem(me + k, lat_count), field),
                            device_id_type=pl.DeviceIdType.MESH)
        return c

    def greet_other(k, c):
        pl.semaphore_signal(barrier, inc=1, device_id=(lax.rem(me + k, lat_count), other),
                            device_id_type=pl.DeviceIdType.MESH)
        return c

    lax.fori_loop(1, lat_count, greet_own, 0)
    lax.fori_loop(0, lat_count, greet_other, 0)

    nord = table_ref.shape[0] // 2
    loads[0].wait()
    loads[1].wait()
    by_slot = orders_ref[...]
    tiled = jnp.concatenate([by_slot] * (2 * lat_count), axis=0)
    here = iota((all_rows, lat_count), 1) == iota((all_rows, lat_count), 0) // block
    order_col = jnp.sum(jnp.where(here, tiled, 0), axis=1, keepdims=True)
    mode_total = lat_count * per_dev
    mode_row = iota((tail_rows, mode_total), 0)
    mode_here = iota((tail_rows, mode_total), 1) == mode_row // tail * per_dev + mode_row % per_dev
    mode_col = jnp.sum(jnp.where(mode_here, modes_ref[0:1, :], 0), axis=1, keepdims=True)
    deg_col = jnp.sum(jnp.where(mode_here, modes_ref[1:2, :], 0), axis=1, keepdims=True)
    my_orders = jnp.sum(
        jnp.where(iota((slots, lat_count), 1) == me, by_slot, 0), axis=1, keepdims=True
    )
    group_of = (iota((lat_count, all_rows), 1) // block == iota((lat_count, all_rows), 0))
    by_lane = mm(by_slot.astype(F32).astype(BF), group_of.astype(F32).astype(BF))
    slot_of = iota((slots, all_rows), 1) % slots == iota((slots, all_rows), 0)
    row_order = jnp.sum(jnp.where(slot_of, by_lane, 0.0), axis=0, keepdims=True).astype(jnp.int32)
    parity_row = iota((all_rows, 1), 0) // slots % 2
    want = jnp.where(order_col >= 0, order_col + nord * parity_row, -1)
    onehot = (iota((all_rows, 2 * nord), 1) == want).astype(F32).astype(BF)
    loads[2].wait()
    dft = mm(onehot, table_ref[...]).astype(BF)
    rho = iota((tail_rows, 1), 0) % tail
    row_parity = iota((1, all_rows), 1) // slots % 2
    mode_parity = (deg_col - mode_col) % 2
    match = (mode_col == row_order) & (mode_parity == row_parity)
    tail_acc = jnp.zeros((tail_rows, width), F32)
    zero_x = jnp.zeros((snap, 2 * lon), BF)
    loads[3].wait()
    for j in range(pairs):
        xj = jnp.concatenate([x_ref[:, j, 0, :], x_ref[:, j, 1, :]], axis=1)
        both = jnp.concatenate(
            [jnp.concatenate([xj, zero_x], axis=1), jnp.concatenate([zero_x, xj], axis=1)], axis=0
        )
        part = (mm_nt(dft, both) * (1.0 / math.sqrt(lon))).astype(BF)
        send[:, j * block:(j + 1) * block, :] = part.reshape(lat_count, block, width)
        mine = match & (rho // per_dev == j)
        tail_acc = tail_acc + mm(mine.astype(F32).astype(BF), part)
    at_degree = (iota((tail_rows, degs), 1) == deg_col) & (rho >= used) & (rho < used + per_dev)
    loads[4].wait()
    basis_acc = jnp.zeros((tail_rows, pair_total), F32)
    for s in range(slots):
        pick = at_degree & (mode_col == my_orders[s:s + 1, :])
        basis_acc = basis_acc + mm_nt(pick.astype(F32).astype(BF), basis_ref[s])
    wide = jnp.concatenate(
        [basis_acc, jnp.zeros((tail_rows, width - pair_total), F32)], axis=1
    )
    tail_all = (tail_acc + wide).astype(BF)
    tail_send[...] = tail_all.reshape(lat_count, tail, width)

    pl.semaphore_wait(barrier, 2 * lat_count - 1)

    def whole(src, dst, count, one_send_sem, one_recv_sem):
        return pltpu.make_async_remote_copy(
            src_ref=src.at[pl.ds(0, count)], dst_ref=dst.at[pl.ds(0, count)],
            send_sem=one_send_sem, recv_sem=one_recv_sem,
            device_id=(me, other), device_id_type=pl.DeviceIdType.MESH,
        )

    def block_copy(dst, src):
        return pltpu.make_async_remote_copy(
            src_ref=send.at[dst], dst_ref=recv.at[src],
            send_sem=send_sem, recv_sem=recv_sem,
            device_id=(dst, field), device_id_type=pl.DeviceIdType.MESH,
        )

    def partner(step):
        offset = lat_count // 2 + (1 - 2 * (step % 2)) * ((step + 1) // 2)
        return lax.rem(me + offset, lat_count)

    def tail_copy(dst, src):
        return pltpu.make_async_remote_copy(
            src_ref=tail_send.at[dst], dst_ref=tail_recv.at[src],
            send_sem=tail_send_sem, recv_sem=tail_recv_sem,
            device_id=(dst, field), device_id_type=pl.DeviceIdType.MESH,
        )

    def start_tail(k, c):
        tail_copy(partner(k), me).start()
        return c

    lax.fori_loop(0, lat_count - 1, start_tail, 0)

    def start_block(k, c):
        block_copy(partner(k), me).start()
        return c

    lax.fori_loop(0, lat_count - 1, start_block, 0)
    recv[me] = send[me]
    tail_recv[me] = tail_send[me]

    src_of = iota((width, tail_rows), 1) // tail
    rho_of = iota((width, tail_rows), 1) % tail
    spread = (
        (iota((width, tail_rows), 0) == src_of * pairs + rho_of // per_dev) & (rho_of < used)
    ).astype(F32).astype(BF)
    own_row = iota((per_dev, tail_rows), 0) == iota((per_dev, tail_rows), 1) % tail % per_dev

    k_rows = slots * 2 * pair_total
    for s in range(slots):
        shape = (2 * pair_total, k_rows // 1)
        r = iota((2 * pair_total, 1), 0)
        p = r // pair_total
        j = r % pair_total
        target = j * block + p * slots + s
        perm[s * 2 * pair_total:(s + 1) * 2 * pair_total, :] = (
            iota((2 * pair_total, lat_count * head), 1) == target
        ).astype(F32).astype(BF)
    dup = (iota((2 * degs, degs), 0) // 2 == iota((2 * degs, degs), 1)).astype(F32).astype(BF)
    for s in range(slots):
        order = my_orders[s:s + 1, :]
        deg = iota((2 * degs, pair_total), 0) // 2
        base = mm_nt(dup, basis_ref[s])
        keep = (deg >= order) & (order >= 0)
        odd = (deg - order) % 2
        even_part = jnp.where(keep & (odd == 0), base, 0.0)
        odd_part = jnp.where(keep & (odd == 1), base, 0.0)
        rows[s] = jnp.concatenate([even_part, odd_part], axis=1).astype(BF)
    all_tails = whole(tail_send, tail_recv, lat_count - 1, tail_send_sem, tail_recv_sem)
    all_tails.wait_recv()

    tails = tail_recv[...]
    summed = jnp.sum(tails.astype(F32), axis=0)[used:used + per_dev].astype(BF)
    weights = jnp.where(own_row, mm(summed, spread), 0.0).astype(BF)
    mode_send[...] = mm(weights, tails.reshape(tail_rows, width)).astype(BF)

    def mode_copy(dst, src):
        return pltpu.make_async_remote_copy(
            src_ref=mode_send, dst_ref=mode_recv.at[src],
            send_sem=mode_send_sem, recv_sem=mode_recv_sem,
            device_id=(dst, other), device_id_type=pl.DeviceIdType.MESH,
        )

    def start_mode(k, c):
        mode_copy(partner(k), me).start()
        return c

    lax.fori_loop(0, lat_count, start_mode, 0)

    all_blocks = whole(send, recv, lat_count - 1, send_sem, recv_sem)
    all_blocks.wait_recv()

    heads = recv[...].reshape(lat_count * head, width)
    sorted_rows = mm(perm[...], heads).astype(BF)
    same_r = iota((2 * degs, width), 1) // snap == iota((2 * degs, width), 0) % 2
    for s in range(slots):
        value = mm(rows[s], sorted_rows[s * 2 * pair_total:(s + 1) * 2 * pair_total])
        coef_hbm[s] = jnp.where(same_r, value, 0.0).astype(BF)

    modes = lat_count * per_dev
    expand = (iota((2 * modes, modes), 1) == iota((2 * modes, modes), 0) // 2).astype(F32).astype(BF)

    all_modes = whole(mode_recv, mode_recv, lat_count, mode_send_sem, mode_recv_sem)
    all_modes.wait_recv()
    values = mode_recv[...].reshape(modes, width)
    columns = mm(expand, values)
    u_match = iota((2 * modes, width), 1) // snap == iota((2 * modes, width), 0) % 2
    masked = jnp.where(u_match, columns, 0.0)
    mean = jnp.sum(masked, axis=1, keepdims=True) * (1.0 / snap)
    centered = jnp.where(u_match, masked - mean, 0.0)
    twice_ref[...] = (centered + pltpu.roll(centered, snap, 1)).astype(BF)

    all_blocks.wait_send()
    all_tails.wait_send()
    all_modes.wait_send()


def dft_constant(nord, lon):
    angles = (np.outer(np.arange(nord), np.arange(lon)) % lon) * (2.0 * math.pi / lon)
    cosine, sine = np.cos(angles), -np.sin(angles)
    even = np.concatenate([cosine, cosine, sine, sine], axis=1)
    odd = np.concatenate([cosine, -cosine, sine, -sine], axis=1)
    return np.concatenate([even, odd], axis=0).astype(np.float32).astype(BF)


def fused(lat_count, tail, fields_grid, basis, order_table, panel_modes):
    _, snap, _, pairs, lon = fields_grid.shape
    slots, pair_total, degs = basis.shape
    modes = panel_modes.shape[1]
    per_dev = modes // lat_count
    width = 2 * snap
    block = 2 * slots
    head = pairs * block
    x = fields_grid[0].transpose(0, 2, 1, 3)
    table = jnp.asarray(dft_constant(degs, lon))
    vmem = pl.BlockSpec(memory_space=pltpu.VMEM)
    body = functools.partial(kernel, lat_count, snap, pairs, lon, slots, degs, per_dev, tail)
    coef, twice = pl.pallas_call(
        body,
        out_shape=(
            jax.ShapeDtypeStruct((slots, 2 * degs, width), BF),
            jax.ShapeDtypeStruct((2 * modes, width), BF),
        ),
        in_specs=[pl.BlockSpec(memory_space=pl.ANY)] * 5,
        out_specs=(vmem, vmem),
        scratch_shapes=[
            pltpu.VMEM(x.shape, BF),
            pltpu.VMEM(basis.shape, BF),
            pltpu.VMEM(table.shape, BF),
            pltpu.VMEM((slots, lat_count), jnp.int32),
            pltpu.VMEM(panel_modes.shape, jnp.int32),
            pltpu.SemaphoreType.DMA((5,)),
            pltpu.VMEM((lat_count, head, width), BF),
            pltpu.VMEM((lat_count, head, width), BF),
            pltpu.VMEM((lat_count, tail, width), BF),
            pltpu.VMEM((lat_count, tail, width), BF),
            pltpu.VMEM((per_dev, width), BF),
            pltpu.VMEM((lat_count, per_dev, width), BF),
            pltpu.VMEM((slots * 2 * pair_total, lat_count * head), BF),
            pltpu.VMEM((slots, 2 * degs, 2 * pair_total), BF),
            pltpu.SemaphoreType.DMA,
            pltpu.SemaphoreType.DMA,
            pltpu.SemaphoreType.DMA,
            pltpu.SemaphoreType.DMA,
            pltpu.SemaphoreType.DMA,
            pltpu.SemaphoreType.DMA,
        ],
        compiler_params=pltpu.CompilerParams(
            collective_id=0, has_side_effects=True, vmem_limit_bytes=52 * 1024 * 1024
        ),
    )(*[pltpu.with_memory_space_constraint(v, pltpu.HBM) for v in (x, basis, table, order_table.T, panel_modes)])
    panel = lax.dot_general(
        coef.reshape(slots * 2 * degs, width), twice, NT, preferred_element_type=F32
    ) * (1.0 / (snap - 1))
    return panel.astype(BF).reshape(1, slots, 2 * degs, 2 * modes)


def dft_table(orders, lon_count):
    valid_slot = orders >= 0
    safe_orders = jnp.maximum(orders, 0)
    products = lax.broadcasted_iota(jnp.int32, (lon_count, 1), 0) * safe_orders[None, :] % lon_count
    angles = products.astype(jnp.float32) * (2.0 * math.pi / lon_count)
    cosine = jnp.where(valid_slot[None, :], jnp.cos(angles), 0.0).astype(jnp.bfloat16)
    sine_table = jnp.where(valid_slot[None, :], -jnp.sin(angles), 0.0).astype(jnp.bfloat16)
    return jnp.stack([cosine, sine_table], axis=1)


def local(fields_grid, basis, order_table, panel_modes):
    grid_one = fields_grid[0]
    snap_count = grid_one.shape[0]
    pair_count = grid_one.shape[2]
    lon_count = grid_one.shape[3]
    slot_count = order_table.shape[1]
    deg_count = basis.shape[2]
    pair_total = basis.shape[1]
    mode_count = panel_modes.shape[1]
    orders = order_table.reshape(-1)
    slot_all = orders.shape[0]
    dft = dft_table(orders, lon_count)
    fourier = jnp.einsum("thjn,nrk->hkjrt", grid_one, dft, preferred_element_type=jnp.float32) * (
        1.0 / math.sqrt(lon_count)
    )
    fourier = fourier.reshape(2, slot_all, pair_count, 2 * snap_count)
    parity_parts = jnp.stack([fourier[0] + fourier[1], fourier[0] - fourier[1]]).astype(
        jnp.bfloat16
    )
    group_index = lax.axis_index("lat")
    my_orders = lax.dynamic_slice_in_dim(order_table, group_index, 1, 0)[0]
    my_odd = my_orders % 2 == 1
    basis_split = basis.reshape(slot_count, pair_total, deg_count // 2, 2)
    even_rows = basis_split[:, :, :, 0]
    odd_rows = basis_split[:, :, :, 1]
    degree = lax.broadcasted_iota(jnp.int32, (1, deg_count), 1)
    keep_mask = (degree >= my_orders[:, None]) & (my_orders >= 0)[:, None]
    received = lax.all_to_all(parity_parts, "lat", split_axis=1, concat_axis=2, tiled=True)
    first_parity = jnp.where(my_odd[:, None, None], received[1], received[0])
    second = jnp.where(my_odd[:, None, None], received[0], received[1])
    low_degrees = jnp.einsum(
        "sjh,sjc->shc", even_rows, first_parity, preferred_element_type=jnp.float32
    )
    high_degrees = jnp.einsum("sjh,sjc->shc", odd_rows, second, preferred_element_type=jnp.float32)
    joined = jnp.stack([low_degrees, high_degrees], axis=2).reshape(slot_count, deg_count, -1)
    coefficients = jnp.where(keep_mask[:, :, None], joined, 0.0).astype(jnp.bfloat16)
    mode_order = panel_modes[0]
    mode_degree = panel_modes[1]
    onehot = (my_orders[None, :] == mode_order[:, None]).astype(jnp.bfloat16)
    picked = jnp.take(coefficients, mode_degree, axis=1)
    local_values = jnp.einsum("ms,smc->mc", onehot, picked, preferred_element_type=jnp.float32)
    field_index = lax.axis_index("field")
    both_fields = jnp.stack(
        [
            jnp.where(field_index == 0, local_values, 0.0),
            jnp.where(field_index == 1, local_values, 0.0),
        ]
    )
    summed = lax.psum(both_fields, ("lat", "field"))
    other_field = jnp.where(field_index == 0, summed[1], summed[0]).astype(jnp.bfloat16)
    columns = other_field.astype(jnp.float32).reshape(mode_count * 2, snap_count)
    centered = (columns - jnp.mean(columns, axis=1, keepdims=True)).astype(jnp.bfloat16)
    coef_rows = coefficients.reshape(slot_count * deg_count * 2, snap_count)
    panel_values = lax.dot_general(
        coef_rows, centered, (((1,), (1,)), ((), ())), preferred_element_type=jnp.float32
    )
    panel_values = panel_values * (1.0 / (snap_count - 1))
    return panel_values.astype(jnp.bfloat16).reshape(1, slot_count, 2 * deg_count, 2 * mode_count)


def device_program(lat_count, fields_grid, basis, order_table, panel_modes):
    pairs, snap = fields_grid.shape[3], fields_grid.shape[1]
    slots, pair_total, _ = basis.shape
    modes = panel_modes.shape[1]
    per_dev = modes // lat_count
    tail = (pairs + 1) * per_dev if per_dev else 0
    rows = slots * 2 * pair_total
    fits = (
        modes % lat_count == 0
        and lat_count % 2 == 0
        and tail == 2 * slots
        and tail % 16 == 0
        and 2 * snap == 128
        and slots == 8
        and basis.shape[2] <= 256
        and pair_total <= 2 * snap
        and rows * rows * 2 <= 8 * 1024 * 1024
    )
    if fits:
        return fused(lat_count, tail, fields_grid, basis, order_table, panel_modes)
    return local(fields_grid, basis, order_table, panel_modes)


def solution(mesh):
    placed = (P("field", None, None, "lat", None), P("lat", None, None), P(), P())
    return jax.shard_map(
        functools.partial(device_program, mesh.shape["lat"]),
        mesh=mesh, in_specs=placed, out_specs=P("field", "lat", None, None), check_vma=False,
    )
```

```python
import functools
import math

import jax
import jax.numpy as jnp
import numpy as np
from jax import lax
from jax.experimental import pallas as pl
from jax.experimental.pallas import tpu as pltpu
from jax.sharding import PartitionSpec as P

BF = jnp.bfloat16
F32 = jnp.float32
NT = (((1,), (1,)), ((), ()))


def iota(shape, dim):
    return lax.broadcasted_iota(jnp.int32, shape, dim)


def mm(a, b):
    return jnp.dot(a, b, preferred_element_type=F32)


def mm_nt(a, b):
    return lax.dot_general(a, b, NT, preferred_element_type=F32)


def kernel(
    lat_count, snap, pairs, lon, slots, degs, per_dev, tail,
    x_hbm, basis_hbm, table_hbm, orders_hbm, modes_hbm,
    coef_hbm, twice_ref,
    x_ref, basis_ref, table_ref, orders_ref, modes_ref, load_sem,
    send, recv, tail_send, tail_recv, mode_send, mode_recv, perm, rows,
    send_sem, recv_sem, tail_send_sem, tail_recv_sem, mode_send_sem, mode_recv_sem,
):
    me = lax.axis_index("lat")
    field = lax.axis_index("field")
    other = 1 - field
    pair_total = lat_count * pairs
    width = 2 * snap
    block = 2 * slots
    head = pairs * block
    all_rows = lat_count * block
    tail_rows = lat_count * tail
    used = pairs * per_dev

    loads = [
        pltpu.make_async_copy(src, dst, load_sem.at[at])
        for at, (src, dst) in enumerate([
            (orders_hbm, orders_ref), (modes_hbm, modes_ref), (table_hbm, table_ref),
            (x_hbm, x_ref), (basis_hbm, basis_ref),
        ])
    ]
    for load in loads:
        load.start()

    barrier = pltpu.get_barrier_semaphore()

    def greet_own(k, c):
        pl.semaphore_signal(barrier, inc=1, device_id=(lax.rem(me + k, lat_count), field),
                            device_id_type=pl.DeviceIdType.MESH)
        return c

    def greet_other(k, c):
        pl.semaphore_signal(barrier, inc=1, device_id=(lax.rem(me + k, lat_count), other),
                            device_id_type=pl.DeviceIdType.MESH)
        return c

    lax.fori_loop(1, lat_count, greet_own, 0)
    lax.fori_loop(0, lat_count, greet_other, 0)

    nord = table_ref.shape[0] // 2
    loads[0].wait()
    loads[1].wait()
    by_slot = orders_ref[...]
    tiled = jnp.concatenate([by_slot] * (2 * lat_count), axis=0)
    here = iota((all_rows, lat_count), 1) == iota((all_rows, lat_count), 0) // block
    order_col = jnp.sum(jnp.where(here, tiled, 0), axis=1, keepdims=True)
    mode_total = lat_count * per_dev
    mode_row = iota((tail_rows, mode_total), 0)
    mode_here = iota((tail_rows, mode_total), 1) == mode_row // tail * per_dev + mode_row % per_dev
    mode_col = jnp.sum(jnp.where(mode_here, modes_ref[0:1, :], 0), axis=1, keepdims=True)
    deg_col = jnp.sum(jnp.where(mode_here, modes_ref[1:2, :], 0), axis=1, keepdims=True)
    my_orders = jnp.sum(
        jnp.where(iota((slots, lat_count), 1) == me, by_slot, 0), axis=1, keepdims=True
    )
    group_of = (iota((lat_count, all_rows), 1) // block == iota((lat_count, all_rows), 0))
    by_lane = mm(by_slot.astype(F32).astype(BF), group_of.astype(F32).astype(BF))
    slot_of = iota((slots, all_rows), 1) % slots == iota((slots, all_rows), 0)
    row_order = jnp.sum(jnp.where(slot_of, by_lane, 0.0), axis=0, keepdims=True).astype(jnp.int32)
    parity_row = iota((all_rows, 1), 0) // slots % 2
    want = jnp.where(order_col >= 0, order_col + nord * parity_row, -1)
    onehot = (iota((all_rows, 2 * nord), 1) == want).astype(F32).astype(BF)
    loads[2].wait()
    dft = mm(onehot, table_ref[...]).astype(BF)
    rho = iota((tail_rows, 1), 0) % tail
    row_parity = iota((1, all_rows), 1) // slots % 2
    mode_parity = (deg_col - mode_col) % 2
    match = (mode_col == row_order) & (mode_parity == row_parity)
    tail_acc = jnp.zeros((tail_rows, width), F32)
    zero_x = jnp.zeros((snap, 2 * lon), BF)
    parts = []
    loads[3].wait()
    for j in range(pairs):
        xj = jnp.concatenate([x_ref[:, j, 0, :], x_ref[:, j, 1, :]], axis=1)
        both = jnp.concatenate(
            [jnp.concatenate([xj, zero_x], axis=1), jnp.concatenate([zero_x, xj], axis=1)], axis=0
        )
        part = (mm_nt(dft, both) * (1.0 / math.sqrt(lon))).astype(BF)
        send[:, j * block:(j + 1) * block, :] = part.reshape(lat_count, block, width)
        parts.append(part)
    picked = mm(match.astype(F32).astype(BF), jnp.concatenate(parts, axis=1))
    for j in range(pairs):
        tail_acc = jnp.where(rho // per_dev == j, picked[:, j * width:(j + 1) * width], tail_acc)
    at_degree = (iota((tail_rows, degs), 1) == deg_col) & (rho >= used) & (rho < used + per_dev)
    loads[4].wait()
    basis_acc = jnp.zeros((tail_rows, pair_total), F32)
    for s in range(slots):
        pick = at_degree & (mode_col == my_orders[s:s + 1, :])
        basis_acc = basis_acc + mm_nt(pick.astype(F32).astype(BF), basis_ref[s])
    wide = jnp.concatenate(
        [basis_acc, jnp.zeros((tail_rows, width - pair_total), F32)], axis=1
    )
    tail_all = (tail_acc + wide).astype(BF)
    tail_send[...] = tail_all.reshape(lat_count, tail, width)

    pl.semaphore_wait(barrier, 2 * lat_count - 1)

    def whole(src, dst, count, one_send_sem, one_recv_sem):
        return pltpu.make_async_remote_copy(
            src_ref=src.at[pl.ds(0, count)], dst_ref=dst.at[pl.ds(0, count)],
            send_sem=one_send_sem, recv_sem=one_recv_sem,
            device_id=(me, other), device_id_type=pl.DeviceIdType.MESH,
        )

    def block_copy(dst, src):
        return pltpu.make_async_remote_copy(
            src_ref=send.at[dst], dst_ref=recv.at[src],
            send_sem=send_sem, recv_sem=recv_sem,
            device_id=(dst, field), device_id_type=pl.DeviceIdType.MESH,
        )

    def tail_copy(dst, src):
        return pltpu.make_async_remote_copy(
            src_ref=tail_send.at[dst], dst_ref=tail_recv.at[src],
            send_sem=tail_send_sem, recv_sem=tail_recv_sem,
            device_id=(dst, field), device_id_type=pl.DeviceIdType.MESH,
        )

    def start_tail(k, c):
        tail_copy(lax.rem(me + k, lat_count), me).start()
        return c

    lax.fori_loop(1, lat_count, start_tail, 0)

    def start_block(k, c):
        block_copy(lax.rem(me + k, lat_count), me).start()
        return c

    lax.fori_loop(1, lat_count, start_block, 0)
    recv[me] = send[me]
    tail_recv[me] = tail_send[me]

    src_of = iota((width, tail_rows), 1) // tail
    rho_of = iota((width, tail_rows), 1) % tail
    spread = (
        (iota((width, tail_rows), 0) == src_of * pairs + rho_of // per_dev) & (rho_of < used)
    ).astype(F32).astype(BF)
    own_row = iota((per_dev, tail_rows), 0) == iota((per_dev, tail_rows), 1) % tail % per_dev

    k_rows = slots * 2 * pair_total
    for s in range(slots):
        shape = (2 * pair_total, k_rows // 1)
        r = iota((2 * pair_total, 1), 0)
        p = r // pair_total
        j = r % pair_total
        target = j * block + p * slots + s
        perm[s * 2 * pair_total:(s + 1) * 2 * pair_total, :] = (
            iota((2 * pair_total, lat_count * head), 1) == target
        ).astype(F32).astype(BF)
    dup = (iota((2 * degs, degs), 0) // 2 == iota((2 * degs, degs), 1)).astype(F32).astype(BF)
    for s in range(slots):
        order = my_orders[s:s + 1, :]
        deg = iota((2 * degs, pair_total), 0) // 2
        base = mm_nt(dup, basis_ref[s])
        keep = (deg >= order) & (order >= 0)
        odd = (deg - order) % 2
        even_part = jnp.where(keep & (odd == 0), base, 0.0)
        odd_part = jnp.where(keep & (odd == 1), base, 0.0)
        rows[s] = jnp.concatenate([even_part, odd_part], axis=1).astype(BF)
    all_tails = whole(tail_send, tail_recv, lat_count - 1, tail_send_sem, tail_recv_sem)
    all_tails.wait_recv()

    tails = tail_recv[...]
    summed = jnp.sum(tails.astype(F32), axis=0)[used:used + per_dev].astype(BF)
    weights = jnp.where(own_row, mm(summed, spread), 0.0).astype(BF)
    mode_send[...] = mm(weights, tails.reshape(tail_rows, width)).astype(BF)

    def mode_copy(dst, src):
        return pltpu.make_async_remote_copy(
            src_ref=mode_send, dst_ref=mode_recv.at[src],
            send_sem=mode_send_sem, recv_sem=mode_recv_sem,
            device_id=(dst, other), device_id_type=pl.DeviceIdType.MESH,
        )

    def start_mode(k, c):
        mode_copy(lax.rem(me + k, lat_count), me).start()
        return c

    lax.fori_loop(0, lat_count, start_mode, 0)

    all_blocks = whole(send, recv, lat_count - 1, send_sem, recv_sem)
    all_blocks.wait_recv()

    heads = recv[...].reshape(lat_count * head, width)
    sorted_rows = mm(perm[...], heads).astype(BF)
    same_r = iota((2 * degs, width), 1) // snap == iota((2 * degs, width), 0) % 2
    for s in range(slots):
        value = mm(rows[s], sorted_rows[s * 2 * pair_total:(s + 1) * 2 * pair_total])
        coef_hbm[s] = jnp.where(same_r, value, 0.0).astype(BF)

    modes = lat_count * per_dev
    expand = (iota((2 * modes, modes), 1) == iota((2 * modes, modes), 0) // 2).astype(F32).astype(BF)

    all_modes = whole(mode_recv, mode_recv, lat_count, mode_send_sem, mode_recv_sem)
    all_modes.wait_recv()
    values = mode_recv[...].reshape(modes, width)
    columns = mm(expand, values)
    u_match = iota((2 * modes, width), 1) // snap == iota((2 * modes, width), 0) % 2
    masked = jnp.where(u_match, columns, 0.0)
    mean = jnp.sum(masked, axis=1, keepdims=True) * (1.0 / snap)
    centered = jnp.where(u_match, masked - mean, 0.0)
    twice_ref[...] = (centered + pltpu.roll(centered, snap, 1)).astype(BF)

    all_blocks.wait_send()
    all_tails.wait_send()
    all_modes.wait_send()


def dft_constant(nord, lon):
    angles = (np.outer(np.arange(nord), np.arange(lon)) % lon) * (2.0 * math.pi / lon)
    cosine, sine = np.cos(angles), -np.sin(angles)
    even = np.concatenate([cosine, cosine, sine, sine], axis=1)
    odd = np.concatenate([cosine, -cosine, sine, -sine], axis=1)
    return np.concatenate([even, odd], axis=0).astype(np.float32).astype(BF)


def fused(lat_count, tail, fields_grid, basis, order_table, panel_modes):
    _, snap, _, pairs, lon = fields_grid.shape
    slots, pair_total, degs = basis.shape
    modes = panel_modes.shape[1]
    per_dev = modes // lat_count
    width = 2 * snap
    block = 2 * slots
    head = pairs * block
    x = fields_grid[0].transpose(0, 2, 1, 3)
    table = jnp.asarray(dft_constant(degs, lon))
    vmem = pl.BlockSpec(memory_space=pltpu.VMEM)
    body = functools.partial(kernel, lat_count, snap, pairs, lon, slots, degs, per_dev, tail)
    coef, twice = pl.pallas_call(
        body,
        out_shape=(
            jax.ShapeDtypeStruct((slots, 2 * degs, width), BF),
            jax.ShapeDtypeStruct((2 * modes, width), BF),
        ),
        in_specs=[pl.BlockSpec(memory_space=pl.ANY)] * 5,
        out_specs=(vmem, vmem),
        scratch_shapes=[
            pltpu.VMEM(x.shape, BF),
            pltpu.VMEM(basis.shape, BF),
            pltpu.VMEM(table.shape, BF),
            pltpu.VMEM((slots, lat_count), jnp.int32),
            pltpu.VMEM(panel_modes.shape, jnp.int32),
            pltpu.SemaphoreType.DMA((5,)),
            pltpu.VMEM((lat_count, head, width), BF),
            pltpu.VMEM((lat_count, head, width), BF),
            pltpu.VMEM((lat_count, tail, width), BF),
            pltpu.VMEM((lat_count, tail, width), BF),
            pltpu.VMEM((per_dev, width), BF),
            pltpu.VMEM((lat_count, per_dev, width), BF),
            pltpu.VMEM((slots * 2 * pair_total, lat_count * head), BF),
            pltpu.VMEM((slots, 2 * degs, 2 * pair_total), BF),
            pltpu.SemaphoreType.DMA,
            pltpu.SemaphoreType.DMA,
            pltpu.SemaphoreType.DMA,
            pltpu.SemaphoreType.DMA,
            pltpu.SemaphoreType.DMA,
            pltpu.SemaphoreType.DMA,
        ],
        compiler_params=pltpu.CompilerParams(
            collective_id=0, has_side_effects=True, vmem_limit_bytes=52 * 1024 * 1024
        ),
    )(*[pltpu.with_memory_space_constraint(v, pltpu.HBM) for v in (x, basis, table, order_table.T, panel_modes)])
    panel = lax.dot_general(
        coef.reshape(slots * 2 * degs, width), twice, NT, preferred_element_type=F32
    ) * (1.0 / (snap - 1))
    return panel.astype(BF).reshape(1, slots, 2 * degs, 2 * modes)


def dft_table(orders, lon_count):
    valid_slot = orders >= 0
    safe_orders = jnp.maximum(orders, 0)
    products = lax.broadcasted_iota(jnp.int32, (lon_count, 1), 0) * safe_orders[None, :] % lon_count
    angles = products.astype(jnp.float32) * (2.0 * math.pi / lon_count)
    cosine = jnp.where(valid_slot[None, :], jnp.cos(angles), 0.0).astype(jnp.bfloat16)
    sine_table = jnp.where(valid_slot[None, :], -jnp.sin(angles), 0.0).astype(jnp.bfloat16)
    return jnp.stack([cosine, sine_table], axis=1)


def local(fields_grid, basis, order_table, panel_modes):
    grid_one = fields_grid[0]
    snap_count = grid_one.shape[0]
    pair_count = grid_one.shape[2]
    lon_count = grid_one.shape[3]
    slot_count = order_table.shape[1]
    deg_count = basis.shape[2]
    pair_total = basis.shape[1]
    mode_count = panel_modes.shape[1]
    orders = order_table.reshape(-1)
    slot_all = orders.shape[0]
    dft = dft_table(orders, lon_count)
    fourier = jnp.einsum("thjn,nrk->hkjrt", grid_one, dft, preferred_element_type=jnp.float32) * (
        1.0 / math.sqrt(lon_count)
    )
    fourier = fourier.reshape(2, slot_all, pair_count, 2 * snap_count)
    parity_parts = jnp.stack([fourier[0] + fourier[1], fourier[0] - fourier[1]]).astype(
        jnp.bfloat16
    )
    group_index = lax.axis_index("lat")
    my_orders = lax.dynamic_slice_in_dim(order_table, group_index, 1, 0)[0]
    my_odd = my_orders % 2 == 1
    basis_split = basis.reshape(slot_count, pair_total, deg_count // 2, 2)
    even_rows = basis_split[:, :, :, 0]
    odd_rows = basis_split[:, :, :, 1]
    degree = lax.broadcasted_iota(jnp.int32, (1, deg_count), 1)
    keep_mask = (degree >= my_orders[:, None]) & (my_orders >= 0)[:, None]
    received = lax.all_to_all(parity_parts, "lat", split_axis=1, concat_axis=2, tiled=True)
    first_parity = jnp.where(my_odd[:, None, None], received[1], received[0])
    second = jnp.where(my_odd[:, None, None], received[0], received[1])
    low_degrees = jnp.einsum(
        "sjh,sjc->shc", even_rows, first_parity, preferred_element_type=jnp.float32
    )
    high_degrees = jnp.einsum("sjh,sjc->shc", odd_rows, second, preferred_element_type=jnp.float32)
    joined = jnp.stack([low_degrees, high_degrees], axis=2).reshape(slot_count, deg_count, -1)
    coefficients = jnp.where(keep_mask[:, :, None], joined, 0.0).astype(jnp.bfloat16)
    mode_order = panel_modes[0]
    mode_degree = panel_modes[1]
    onehot = (my_orders[None, :] == mode_order[:, None]).astype(jnp.bfloat16)
    picked = jnp.take(coefficients, mode_degree, axis=1)
    local_values = jnp.einsum("ms,smc->mc", onehot, picked, preferred_element_type=jnp.float32)
    field_index = lax.axis_index("field")
    both_fields = jnp.stack(
        [
            jnp.where(field_index == 0, local_values, 0.0),
            jnp.where(field_index == 1, local_values, 0.0),
        ]
    )
    summed = lax.psum(both_fields, ("lat", "field"))
    other_field = jnp.where(field_index == 0, summed[1], summed[0]).astype(jnp.bfloat16)
    columns = other_field.astype(jnp.float32).reshape(mode_count * 2, snap_count)
    centered = (columns - jnp.mean(columns, axis=1, keepdims=True)).astype(jnp.bfloat16)
    coef_rows = coefficients.reshape(slot_count * deg_count * 2, snap_count)
    panel_values = lax.dot_general(
        coef_rows, centered, (((1,), (1,)), ((), ())), preferred_element_type=jnp.float32
    )
    panel_values = panel_values * (1.0 / (snap_count - 1))
    return panel_values.astype(jnp.bfloat16).reshape(1, slot_count, 2 * deg_count, 2 * mode_count)


def device_program(lat_count, fields_grid, basis, order_table, panel_modes):
    pairs, snap = fields_grid.shape[3], fields_grid.shape[1]
    slots, pair_total, _ = basis.shape
    modes = panel_modes.shape[1]
    per_dev = modes // lat_count
    tail = (pairs + 1) * per_dev if per_dev else 0
    rows = slots * 2 * pair_total
    fits = (
        modes % lat_count == 0
        and tail == 2 * slots
        and tail % 16 == 0
        and 2 * snap == 128
        and slots == 8
        and basis.shape[2] <= 256
        and pair_total <= 2 * snap
        and rows * rows * 2 <= 8 * 1024 * 1024
    )
    if fits:
        return fused(lat_count, tail, fields_grid, basis, order_table, panel_modes)
    return local(fields_grid, basis, order_table, panel_modes)


def solution(mesh):
    placed = (P("field", None, None, "lat", None), P("lat", None, None), P(), P())
    return jax.shard_map(
        functools.partial(device_program, mesh.shape["lat"]),
        mesh=mesh, in_specs=placed, out_specs=P("field", "lat", None, None), check_vma=False,
    )
```
